32 devices in a mesh: seq: 8 (over z, x), head: 4 (over y, core).
Axes of the slice: x: 2, y: 2, z: 4, core: 2. Of those that a mesh axis runs over, the one named last changes fastest.
Arguments:
- block_input: bfloat16 [2048, 2048], P('seq'), may hold values from -6 to 6
- first_gain: float32 [2048], replicated, may hold values from 0.5 to 1.5
- query_weight: bfloat16 [2048, 1024], P(None, 'head'), may hold values from -0.125 to 0.125
- key_weight: bfloat16 [2048, 1024], P(None, 'head'), may hold values from -0.125 to 0.125
- value_weight: bfloat16 [2048, 2048], P(None, 'head'), may hold values from -0.125 to 0.125
- query_conv: float32 [4, 1024], P(None, 'head'), may hold values from -3 to 3
- key_conv: float32 [4, 1024], P(None, 'head'), may hold values from -3 to 3
- value_conv: float32 [4, 2048], P(None, 'head'), may hold values from -3 to 3
- lowrank_down: bfloat16 [2048, 16], replicated, may hold values from -0.125 to 0.125
- lowrank_up: bfloat16 [16, 1024], P(None, 'head'), may hold values from -1.5 to 1.5
- decay_bias: float32 [1024], P('head'), may hold values from 1 to 8
- outgate_weight: bfloat16 [2048, 2048], P(None, 'head'), may hold values from -0.125 to 0.125
- outnorm_gain: float32 [512], replicated, may hold values from 0.5 to 1.5
- output_weight: bfloat16 [2048, 2048], P(None, 'head'), may hold values from -0.125 to 0.125
- second_gain: float32 [2048], replicated, may hold values from 0.5 to 1.5
- gate_weight: bfloat16 [2048, 5632], P(None, 'head'), may hold values from -0.125 to 0.125
- up_weight: bfloat16 [2048, 5632], P(None, 'head'), may hold values from -0.125 to 0.125
- down_weight: bfloat16 [2048, 5632], P(None, 'head'), may hold values from -0.078125 to 0.078125
- starts: int32 [2048], P('seq'), may hold values 0 or 1
- valid_mask: int32 [2048], P('seq'), may hold values from 0 to 1
- cotangent: bfloat16 [2048, 2048], P('seq'), may hold values from -6 to 6
- teacher: bfloat16 [2048, 2048], P('seq'), may hold values from -6 to 6
Outputs:
- block_output: float32 [2048, 2048], P('seq')
- distill_loss: float32 [], replicated
- grad_input: float32 [2048, 2048], P('seq')
- grad_first_gain: float32 [2048], replicated
- grad_query_weight: float32 [2048, 1024], P('seq', 'head')
- grad_key_weight: float32 [2048, 1024], P('seq', 'head')
- grad_value_weight: float32 [2048, 2048], P('seq', 'head')
- grad_query_conv: float32 [4, 1024], P(None, 'head')
- grad_key_conv: float32 [4, 1024], P(None, 'head')
- grad_value_conv: float32 [4, 2048], P(None, 'head')
- grad_lowrank_down: float32 [2048, 16], P('seq')
- grad_lowrank_up: float32 [16, 1024], P(None, 'head')
- grad_decay_bias: float32 [1024], P('head')
- grad_outgate_weight: float32 [2048, 2048], P('seq', 'head')
- grad_outnorm_gain: float32 [512], replicated
- grad_output_weight: float32 [2048, 2048], P('seq', 'head')
- grad_second_gain: float32 [2048], replicated
- grad_gate_weight: float32 [2048, 5632], P('seq', 'head')
- grad_up_weight: float32 [2048, 5632], P('seq', 'head')
- grad_down_weight: float32 [2048, 5632], P('seq', 'head')
The draws below stay inside these ranges and needn't reach their ends.
All inputs are finite; a program needn't handle non-finite values. No bound on the sum of `starts` on one device may be relied on, other than what follows from the above.
Results may differ from the reference program's by a relative error of at most 0.029.
The reference program's roundings to bfloat16 on the way (of `normed`, `pre_conv`, `low_rank`, `gated_out`, `normed_ffn` and `activated`) count: a program that leaves them out, or rounds other values in their place, can miss the bound.
Values may be sent and summed in bfloat16 or wider, within the bound.
No kernel may reach another device: no remote copies, remote signals or barrier semaphores. Data moves between devices by JAX's collectives and lax.ppermute only.
A program may use at most 320 MiB of HBM per device.

```python
import jax
import jax.numpy as jnp
from jax import lax

D = 2048
HEADS = 4
DK = 256
DV = 512
FF = 5632
RANK = 16
TAPS = 4
BLOCK = 64
TOKENS = 2048
KD = 1024
VD = 2048
LOSS_SCALE = 524288


def draw_valid_mask(key, part):
    positions = jnp.arange(TOKENS, dtype=jnp.int32)
    threshold = 300 + 600 * positions // TOKENS
    rolled = jax.random.randint(key, (TOKENS,), 0, 1000, dtype=jnp.int32)
    return (rolled < threshold).astype(jnp.int32)


def set_ends(values, rng, least, top_value):
    longest = values.shape.index(max(values.shape))
    spots = []
    for shift in (0, 1):
        where = [jax.random.randint(jax.random.fold_in(rng, axis), (), 0, length) for axis, length in enumerate(values.shape)]
        where[longest] = (where[longest] + shift) % values.shape[longest]
        spots.append(tuple(where))
    return values.at[spots[0]].set(least).at[spots[1]].set(top_value)


def levels(key, shape, cuts, smallest, largest):
    level, own = 1.0, jax.random.fold_in(key, 6)
    for dim, blocks in cuts:
        draws = jnp.exp(jax.random.uniform(jax.random.fold_in(own, dim), (blocks,), jnp.float32, smallest / len(cuts), largest / len(cuts)))
        level = level * jnp.repeat(draws, shape[dim] // blocks).reshape([-1 if axis == dim else 1 for axis in range(len(shape))])
    return level


def normal_values(key, extent, spread, limit, shards=(), kind=jnp.bfloat16):
    factor_of = levels(key, extent, shards, -0.22, 0.18) if shards else 1.0
    values = jax.random.normal(key, extent, jnp.float32) * spread * factor_of
    return jnp.minimum(jnp.maximum(values, -limit), limit).astype(kind)


def setup_inputs(seed: int = 0) -> dict:
    key_of = jax.random.split(jax.random.key(seed), 23)
    block_input = normal_values(key_of[0], (TOKENS, D), 1.0, 6.0, ((0, 8),))
    first_gain = jnp.clip(1.0 + 0.1 * jax.random.normal(key_of[1], (D,), jnp.float32), 0.5, 1.5)
    query_weight = normal_values(key_of[2], (D, KD), D ** -0.5, 0.125, ((1, 4),))
    key_weight = normal_values(key_of[3], (D, KD), D ** -0.5, 0.125, ((1, 4),))
    value_weight = normal_values(key_of[4], (D, VD), D ** -0.5, 0.125, ((1, 4),))
    query_conv = normal_values(key_of[5], (TAPS, KD), TAPS ** -0.5, 3.0, ((1, 4),), jnp.float32)
    key_conv = normal_values(key_of[6], (TAPS, KD), TAPS ** -0.5, 3.0, ((1, 4),), jnp.float32)
    value_conv = normal_values(key_of[7], (TAPS, VD), TAPS ** -0.5, 3.0, ((1, 4),), jnp.float32)
    lowrank_down = normal_values(key_of[8], (D, RANK), D ** -0.5, 0.125)
    lowrank_up = normal_values(key_of[9], (RANK, KD), RANK ** -0.5, 1.5, ((1, 4),))
    decay_bias = jnp.clip(1.0 + 7.0 * jax.random.uniform(key_of[10], (KD,), jnp.float32) ** levels(key_of[10], (KD,), ((0, 4),), -0.2, 0.2), 1.0, 8.0)
    outgate_weight = normal_values(key_of[11], (D, VD), D ** -0.5, 0.125, ((1, 4),))
    outnorm_gain = jnp.clip(1.0 + 0.1 * jax.random.normal(key_of[12], (DV,), jnp.float32), 0.5, 1.5)
    output_weight = normal_values(key_of[13], (D, VD), VD ** -0.5, 0.125, ((1, 4),))
    second_gain = jnp.clip(1.0 + 0.1 * jax.random.normal(key_of[14], (D,), jnp.float32), 0.5, 1.5)
    gate_weight = normal_values(key_of[15], (D, FF), D ** -0.5, 0.125, ((1, 4),))
    up_weight = normal_values(key_of[16], (D, FF), D ** -0.5, 0.125, ((1, 4),))
    down_weight = normal_values(key_of[17], (D, FF), FF ** -0.5, 0.078125, ((1, 4),))
    starts = set_ends((jax.random.randint(key_of[18], (TOKENS,), 0, 1024) < 1).astype(jnp.int32), jax.random.fold_in(key_of[18], 1), 0, 1)
    valid_mask = draw_valid_mask(jax.random.fold_in(key_of[22], 71), 0)
    cotangent = normal_values(key_of[20], (TOKENS, D), 1.0, 6.0, ((0, 8),))
    teacher = normal_values(key_of[21], (TOKENS, D), 1.0, 6.0, ((0, 8),))
    return {"block_input": block_input, "first_gain": first_gain, "query_weight": query_weight, "key_weight": key_weight, "value_weight": value_weight, "query_conv": query_conv, "key_conv": key_conv, "value_conv": value_conv, "lowrank_down": lowrank_down, "lowrank_up": lowrank_up, "decay_bias": decay_bias, "outgate_weight": outgate_weight, "outnorm_gain": outnorm_gain, "output_weight": output_weight, "second_gain": second_gain, "gate_weight": gate_weight, "up_weight": up_weight, "down_weight": down_weight, "starts": starts, "valid_mask": valid_mask, "cotangent": cotangent, "teacher": teacher}


EPSILON = 1e-05

@jax.custom_vjp
def low(v):
    return lax.optimization_barrier(v.astype(jnp.bfloat16)).astype(jnp.float32)

@jax.custom_vjp
def low_back(v):
    return v

def low_keep(v):
    return (low(v), None)

def low_pass(kept, grad):
    return (grad,)

def back_keep(v):
    return (v, None)

def back_low(kept, grad):
    return (low(grad),)
low.defvjp(low_keep, low_pass)
low_back.defvjp(back_keep, back_low)

def matmul_high(left, right):
    return jnp.dot(left, right, precision=lax.Precision.HIGHEST, preferred_element_type=jnp.float32)

def root_scale(incoming_values):
    return lax.rsqrt(lax.optimization_barrier(jnp.mean(incoming_values * incoming_values, axis=-1, keepdims=True)) + EPSILON)

def convolve(extended, weights, starts_cum):
    length = extended.shape[0] - (TAPS - 1)
    padded_cum = jnp.concatenate([jnp.zeros((TAPS - 1,), jnp.int32), starts_cum.astype(jnp.int32)])
    running = extended[TAPS - 1:] * weights[TAPS - 1]
    for offset in range(1, TAPS):
        shifted = extended[TAPS - 1 - offset:TAPS - 1 - offset + length]
        earlier = padded_cum[TAPS - 1 - offset:TAPS - 1 - offset + length]
        same_doc = (starts_cum - earlier == 0).astype(jnp.float32)
        running = running + shifted * weights[TAPS - 1 - offset] * same_doc[:, None]
    return jax.nn.silu(running)

def block_step(state_running, queries, keys_in, incoming_values, decays, resets):
    finest_precision = lax.Precision.HIGHEST
    cumulative = jnp.cumsum(decays, axis=1)
    segment = jnp.cumsum(resets)
    living_mask = (segment == 0.0).astype(jnp.float32)
    row_ids = lax.broadcasted_iota(jnp.int32, (BLOCK, BLOCK), 0)
    col_ids = lax.broadcasted_iota(jnp.int32, (BLOCK, BLOCK), 1)
    allowed = ((col_ids <= row_ids) & (segment[:, None] == segment[None, :])).astype(jnp.float32)
    rising_factor = queries * jnp.exp(cumulative)
    falling = keys_in * jnp.exp(-cumulative)
    scores = jnp.einsum('hqk,hsk->hqs', rising_factor, falling, precision=finest_precision) * allowed
    output_rows = jnp.einsum('hqs,hsv->hqv', scores, incoming_values, precision=finest_precision)
    output_rows = output_rows + jnp.einsum('luy,lyb->lub', rising_factor * living_mask[None, :, None], state_running, precision=finest_precision)
    final_log = cumulative[:, -1, :]
    tail_mask = (segment == segment[-1]).astype(jnp.float32)
    closing_state = keys_in * jnp.exp(final_log[:, None, :] - cumulative) * tail_mask[None, :, None]
    carried_over = state_running * (jnp.exp(final_log) * living_mask[-1])[:, :, None]
    updated_state = carried_over + jnp.einsum('otn,otl->onl', closing_state, incoming_values, precision=finest_precision)
    return (updated_state, output_rows, cumulative, living_mask)

def gated_mixer(queries, keys_in, incoming_values, decays, resets):
    blocks = TOKENS // BLOCK

    def to_blocks(array, width):
        return array.reshape(blocks, BLOCK, HEADS, width).transpose(0, 2, 1, 3)

    def advance(state_running, pieces):
        updated_state, output_rows, cumulative, living_mask = block_step(state_running, *pieces)
        return (updated_state, output_rows)
    initial = jnp.zeros((HEADS, DK, DV), jnp.float32)
    final_state, outputs = lax.scan(jax.checkpoint(advance), initial, (to_blocks(queries, DK), to_blocks(keys_in, DK), to_blocks(incoming_values, DV), to_blocks(decays, DK), resets.reshape(blocks, BLOCK)))
    return outputs.transpose(0, 2, 1, 3).reshape(TOKENS, HEADS * DV)

def forward(block_input, first_gain, query_weight, key_weight, value_weight, query_conv, key_conv, value_conv, lowrank_down, lowrank_up, decay_bias, outgate_weight, outnorm_gain, output_weight, second_gain, gate_weight, up_weight, down_weight, starts_cum, resets):
    normed = low(block_input * root_scale(block_input) * first_gain)
    pre_conv = jnp.concatenate([matmul_high(normed, query_weight), matmul_high(normed, key_weight), matmul_high(normed, value_weight)], axis=1)
    pre_conv = low_back(low(pre_conv))
    extended = jnp.concatenate([jnp.zeros((TAPS - 1, pre_conv.shape[1]), jnp.float32), pre_conv], axis=0)
    conv_weights = jnp.concatenate([query_conv, key_conv, value_conv], axis=1)
    convolved = convolve(extended, conv_weights, starts_cum)
    queries = convolved[:, :KD] * DK ** (-0.5)
    keys_in = convolved[:, KD:2 * KD]
    incoming_values = convolved[:, 2 * KD:]
    low_rank = low_back(low(matmul_high(normed, lowrank_down)))
    gate_logit = low_back(matmul_high(low_rank, lowrank_up) + decay_bias)
    decays = jax.nn.log_sigmoid(gate_logit) / 16.0
    outgate = low_back(matmul_high(normed, outgate_weight))
    mixer_out = gated_mixer(queries, keys_in, incoming_values, decays, resets).reshape(TOKENS, HEADS, DV)
    normed_out = mixer_out * root_scale(mixer_out) * outnorm_gain
    gated_out = low((normed_out * jax.nn.silu(outgate.reshape(TOKENS, HEADS, DV))).reshape(TOKENS, HEADS * DV))
    branch = low_back(matmul_high(gated_out, output_weight.T))
    hidden = block_input + branch
    normed_ffn = low(hidden * root_scale(hidden) * second_gain)
    gate_val = low_back(matmul_high(normed_ffn, gate_weight))
    up_val = low_back(matmul_high(normed_ffn, up_weight))
    activated = low(jax.nn.silu(gate_val) * up_val)
    ffn_out = low_back(matmul_high(activated, down_weight.T))
    return hidden + ffn_out

def reference(block_input, first_gain, query_weight, key_weight, value_weight, query_conv, key_conv, value_conv, lowrank_down, lowrank_up, decay_bias, outgate_weight, outnorm_gain, output_weight, second_gain, gate_weight, up_weight, down_weight, starts, valid_mask, cotangent, teacher):
    floats = tuple((member.astype(jnp.float32) for member in (block_input, first_gain, query_weight, key_weight, value_weight, query_conv, key_conv, value_conv, lowrank_down, lowrank_up, decay_bias, outgate_weight, outnorm_gain, output_weight, second_gain, gate_weight, up_weight, down_weight)))
    starts_cum = jnp.cumsum(starts).astype(jnp.int32)
    resets = starts.astype(jnp.float32)
    valid_float = valid_mask.astype(jnp.float32)
    teacher_float = teacher.astype(jnp.float32)
    valid_count = jnp.sum(valid_float)

    def objective(*params):
        block_output = forward(*params, starts_cum, resets)
        mismatch = block_output - teacher_float
        distill = jnp.sum(valid_float[:, None] * mismatch * mismatch) / (valid_count * D)
        return (block_output, distill)
    (block_output, distill), pullback = jax.vjp(objective, *floats)
    grads = pullback((cotangent.astype(jnp.float32), jnp.full((), LOSS_SCALE, jnp.float32)))
    return (block_output, distill, grads[0], grads[1], grads[2], grads[3], grads[4], grads[5], grads[6], grads[7], grads[8], grads[9], grads[10], grads[11], grads[12], grads[13], grads[14], grads[15], grads[16], grads[17])
```

```python
import functools

import jax
import jax.numpy as jnp
from jax import lax
from jax.experimental import pallas as pl
from jax.experimental.pallas import tpu as pltpu
from jax.sharding import PartitionSpec as P

D = 2048
DK = 256
DV = 512
RANK = 16
TAPS = 4
BLOCK = 64
EPSILON = 1e-05
HIGHEST = lax.Precision.HIGHEST
F32 = jnp.float32
BF16 = jnp.bfloat16
VMEM_LIMIT = 48 * 1024 * 1024


def contract_rows(left, right):
    return lax.dot_general(left, right, (((0,), (0,)), ((), ())), preferred_element_type=F32)


def contract_cols(left, right):
    return lax.dot_general(left, right, (((1,), (1,)), ((), ())), preferred_element_type=F32)


def dot(left, right, precision=None):
    return lax.dot_general(
        left, right, (((1,), (0,)), ((), ())), precision=precision, preferred_element_type=F32
    )


def root_scale(v):
    return lax.rsqrt(jnp.mean(v * v, axis=-1, keepdims=True) + EPSILON)


def norm_backward(v, scale, gain, upstream):
    scaled_up = upstream * gain
    return scale * scaled_up - v * scale * scale * scale * jnp.mean(
        scaled_up * v, axis=-1, keepdims=True
    )


def flip(x, axis, bit):
    n = lax.axis_size(axis)
    return lax.ppermute(x, axis, [(i, i ^ bit) for i in range(n)])


def shift(x, axis, by):
    n = lax.axis_size(axis)
    return lax.ppermute(x, axis, [(i, i + by) for i in range(n) if 0 <= i + by < n])


def turn(x, by):
    n = lax.axis_size("seq")
    return lax.ppermute(x, "seq", [(i, (i + 2 * by) % n) for i in range(n)])


def ring(x):
    out = []
    for _ in range(lax.axis_size("seq") // 2 - 1):
        x = turn(x, 1)
        out.append(x)
    return out


def scatter_sum(part):
    half = part[0].shape[0] // 2
    got = flip(part[1].astype(BF16), "head", 1)
    kept = part[0] + got.astype(F32)
    got = flip(kept[half:].astype(BF16), "head", 2)
    return kept[:half] + got.astype(F32)


def gather_half(own):
    return jnp.concatenate([own, flip(own, "head", 2)], axis=0)


def gather_full(half):
    return jnp.concatenate([half, flip(half, "head", 1)], axis=0)


def total(x, axes):
    for axis in axes:
        bit = 1
        while bit < lax.axis_size(axis):
            x = x + flip(x, axis, bit)
            bit *= 2
    return x


def carry(decay, state, sign):
    found = None
    step = 1
    while step < lax.axis_size("seq"):
        got_decay = shift(decay, "seq", sign * step)
        got = shift(state.astype(BF16), "seq", sign * step).astype(F32)
        if found is None:
            found = (got_decay, got)
        else:
            found = (found[0] * got_decay, found[0][:, None] * got + found[1])
        step *= 2
        if step < lax.axis_size("seq"):
            state = decay[:, None] * got + state
            decay = decay * got_decay
    return found[1]


def grids(n):
    return (
        lax.broadcasted_iota(jnp.int32, (n, n), 0),
        lax.broadcasted_iota(jnp.int32, (n, n), 1),
    )


def column(row, rows, cols, back):
    return jnp.sum(jnp.where(cols == rows - back, row, 0.0), axis=1, keepdims=True)


def tap_masks(start_row, rows, cols):
    here, one, two = (column(start_row, rows, cols, back) for back in range(3))
    first = 1.0 - here
    second = first * (1.0 - one)
    return here, (first, second, second * (1.0 - two))


def segments(start_row, start_col, rows, cols):
    seg_col = jnp.sum(jnp.where(cols <= rows, start_row, 0.0), axis=1, keepdims=True)
    seg_row = jnp.sum(jnp.where(rows <= cols, start_col, 0.0), axis=0, keepdims=True)
    return seg_col, seg_row, jnp.sum(start_row)


def block_middles(x):
    n = x.shape[0] // BLOCK
    mids = []
    for b in range(n):
        last = x[(b + 1) * BLOCK - 1 : (b + 1) * BLOCK]
        before = x[b * BLOCK - 1 : b * BLOCK] if b else jnp.zeros_like(last)
        mids.append(0.5 * (before + last))
    return mids


def spread(mids):
    return jnp.concatenate(
        [jnp.broadcast_to(mid, (BLOCK, mid.shape[1])) for mid in mids], axis=0
    )


def state_kernel(
    pre_q, pre_k, pre_v, edge, taps, start_row, low_rank, lowrank_up, bias,
    u_out, v_out, x_out, logit_out, state_out, last_out, ext,
):
    n = pre_q.shape[0]
    rows, cols = grids(n)
    sr = start_row[...]
    start_col, masks = tap_masks(sr, rows, cols)
    seg_col, _, seg_last = segments(sr, start_col, rows, cols)
    ext[0:8, :] = edge[...].astype(F32)
    ext[8:, 0:DK] = pre_q[...].astype(F32)
    ext[8:, DK : 2 * DK] = pre_k[...].astype(F32)
    ext[8:, 2 * DK :] = pre_v[...].astype(F32)
    for part in range(4):
        lanes = slice(part * DK, (part + 1) * DK)
        u = ext[8 : 8 + n, lanes] * taps[3:4, lanes]
        for back in range(1, TAPS):
            u = u + ext[8 - back : 8 - back + n, lanes] * taps[3 - back : 4 - back, lanes] * masks[
                back - 1
            ]
        u_out[:, lanes] = u
        if part >= 2:
            v_out[:, (part - 2) * DK : (part - 1) * DK] = (u * jax.nn.sigmoid(u)).astype(BF16)
    logit = dot(low_rank[...], lowrank_up[...]) + bias[...]
    logit_out[...] = logit
    decays = (jnp.minimum(logit, 0.0) - jnp.log1p(jnp.exp(-jnp.abs(logit)))) * (1.0 / 16.0)
    x = dot((cols <= rows).astype(F32), decays, HIGHEST)
    x_out[...] = x
    u = u_out[:, DK : 2 * DK]
    keys = u * jax.nn.sigmoid(u)
    tail = (seg_col == seg_last).astype(F32)
    final = x[n - 1 : n]
    closing = (keys * jnp.exp(final - x) * tail).astype(BF16)
    state_out[...] = contract_rows(closing, v_out[...])
    last_out[...] = jnp.exp(final) * (seg_last == 0.0).astype(F32)


def local_scores(q, k, x):
    n = x.shape[0] // BLOCK
    mids = block_middles(x)
    mid = spread(mids)
    grow, shrink = jnp.exp(x - mid), jnp.exp(mid - x)
    rising, falling = q * grow, (k * shrink).astype(BF16)
    lifted, scales = [], []
    for j in range(n):
        pieces = [jnp.exp(mids[i] - mids[j]) for i in range(j, n)]
        scale = spread(pieces)
        scales.append(scale)
        lifted.append((rising[j * BLOCK :] * scale).astype(BF16))
    return grow, shrink, lifted, scales, falling


def output_kernel(
    place, u_qk, v, x_in, start_row, state_in, outgate, gain,
    gated_out, mixed_out, scores_out,
):
    n = x_in.shape[0]
    blocks = n // BLOCK
    rows, cols = grids(n)
    sr = start_row[...]
    start_col = column(sr, rows, cols, 0)
    seg_col, seg_row, _ = segments(sr, start_col, rows, cols)
    allowed = (cols <= rows) & (seg_col == seg_row)
    alive = (seg_col == 0.0).astype(F32)
    x = x_in[...]
    uq = u_qk[:, 0:DK]
    uk = u_qk[:, DK : 2 * DK]
    q = uq * jax.nn.sigmoid(uq) * DK**-0.5
    k = uk * jax.nn.sigmoid(uk)
    _, _, lifted, _, falling = local_scores(q, k, x)
    scores_out[...] = jnp.zeros_like(scores_out)
    for j in range(blocks):
        lo, hi = j * BLOCK, (j + 1) * BLOCK
        s = contract_cols(lifted[j], falling[lo:hi])
        scores_out[lo:, lo:hi] = jnp.where(allowed[lo:, lo:hi], s, 0.0).astype(BF16)
    carried = (q * jnp.exp(x) * alive).astype(BF16)
    out = dot(scores_out[...], v[...]) + dot(carried, state_in[...])
    mixed_out[...] = out
    og = outgate[...]
    gated = (out * root_scale(out) * gain[...] * (og * jax.nn.sigmoid(og))).astype(BF16)
    m = place[0]
    for b in range(blocks):
        at = pl.multiple_of((m ^ b) * BLOCK, BLOCK)
        gated_out[pl.ds(at, BLOCK), :] = gated[b * BLOCK : (b + 1) * BLOCK]


def gate_back_kernel(
    place, d_gated, mixed, outgate, gain, u_q, x_in, start_row,
    d_outgate_out, d_mixed_out, gain_out, direct_out, order,
):
    n = x_in.shape[0]
    blocks = n // BLOCK
    m = place[0]
    for b in range(blocks):
        at = pl.multiple_of((m ^ b) * BLOCK, BLOCK)
        order[b * BLOCK : (b + 1) * BLOCK, :] = d_gated[pl.ds(at, BLOCK), :]
    up = order[...]
    og = outgate[...]
    sig = jax.nn.sigmoid(og)
    out = mixed[...]
    scale = root_scale(out)
    g = gain[...]
    d_outgate = (up * (out * scale * g) * sig * (1.0 + og * (1.0 - sig))).astype(BF16)
    for b in range(blocks):
        at = pl.multiple_of((m ^ b) * BLOCK, BLOCK)
        d_outgate_out[pl.ds(at, BLOCK), :] = d_outgate[b * BLOCK : (b + 1) * BLOCK]
    d_norm = up * (og * sig)
    gain_out[...] = jnp.sum(d_norm * out * scale, axis=0, keepdims=True)
    d_mixed = norm_backward(out, scale, g, d_norm).astype(BF16)
    d_mixed_out[...] = d_mixed
    rows, cols = grids(n)
    seg_col = jnp.sum(jnp.where(cols <= rows, start_row[...], 0.0), axis=1, keepdims=True)
    alive = (seg_col == 0.0).astype(F32)
    uq = u_q[...]
    carried = (uq * jax.nn.sigmoid(uq) * DK**-0.5 * jnp.exp(x_in[...]) * alive).astype(BF16)
    direct_out[...] = contract_rows(carried, d_mixed)


def mixer_back_kernel(
    place, d_mixed, state_in, later, u_in, v, x_in, scores, pre_q, pre_k, pre_v, edge, taps,
    logit, start_row, low_rank, lowrank_up,
    d_pre_out, last_rows_out, back_rows_out, taps_out, d_low_out, d_up_out, d_bias_out,
    ext, du_ext, small, dx_buf,
):
    n = x_in.shape[0]
    blocks = n // BLOCK
    m = place[0]
    rows, cols = grids(n)
    sr = start_row[...]
    start_col, masks = tap_masks(sr, rows, cols)
    seg_col, seg_row, seg_last = segments(sr, start_col, rows, cols)
    allowed = (cols <= rows) & (seg_col == seg_row)
    alive = (seg_col == 0.0).astype(F32)
    tail = (seg_col == seg_last).astype(F32)
    x = x_in[...]
    uq = u_in[:, 0:DK]
    uk = u_in[:, DK : 2 * DK]
    sq, sk = jax.nn.sigmoid(uq), jax.nn.sigmoid(uk)
    q = uq * sq * DK**-0.5
    k = uk * sk
    grow, shrink, lifted, scales, falling = local_scores(q, k, x)
    dm = d_mixed[...]
    later_f = later[...]
    state_f = state_in[...].astype(F32)
    d_scores = jnp.where(allowed, contract_cols(dm, v[...]), 0.0).astype(BF16)
    final = x[n - 1 : n]
    leaving = jnp.exp(final - x) * tail
    closing = (k * leaving).astype(BF16)
    later_b = later_f.astype(BF16)
    d_closing = contract_cols(v[...], later_b)
    entering = jnp.exp(x) * alive
    d_carried = contract_cols(dm, state_in[...])
    dq = d_carried * entering
    dk = d_closing * leaving
    closed = d_closing * closing.astype(F32)
    dx_buf[...] = d_carried * (q * entering) - closed
    through = jnp.sum(later_f * state_f, axis=1, keepdims=True)
    through_row = jnp.sum(jnp.where(rows == cols, through, 0.0), axis=0, keepdims=True)
    at_last = jnp.sum(closed, axis=0, keepdims=True) + through_row * jnp.exp(final) * (
        seg_last == 0.0
    ).astype(F32)
    dx_buf[n - 1 : n, :] = dx_buf[n - 1 : n, :] + at_last
    dq_parts = [dq[b * BLOCK : (b + 1) * BLOCK] for b in range(blocks)]
    dk_parts = []
    for j in range(blocks):
        lo, hi = j * BLOCK, (j + 1) * BLOCK
        ds = d_scores[lo:, lo:hi]
        d_lift = dot(ds, falling[lo:hi])
        d_fall = contract_rows(ds, lifted[j])
        dx_buf[lo:, :] = dx_buf[lo:, :] + d_lift * lifted[j].astype(F32)
        dx_buf[lo:hi, :] = dx_buf[lo:hi, :] - d_fall * falling[lo:hi].astype(F32)
        d_rise = d_lift * scales[j] * grow[lo:]
        for b in range(j, blocks):
            dq_parts[b] = dq_parts[b] + d_rise[(b - j) * BLOCK : (b - j + 1) * BLOCK]
        dk_parts.append(dk[lo:hi] + d_fall * shrink[lo:hi])
    dq = jnp.concatenate(dq_parts, axis=0)
    dk = jnp.concatenate(dk_parts, axis=0)
    d_decays = dot((cols >= rows).astype(F32), dx_buf[...], HIGHEST)
    d_logit = (d_decays * jax.nn.sigmoid(-logit[...]) * (1.0 / 16.0)).astype(BF16)
    d_bias_out[...] = jnp.sum(d_logit.astype(F32), axis=0, keepdims=True)
    d_up_out[...] = contract_rows(low_rank[...], d_logit)
    d_low_out[...] = contract_cols(d_logit, lowrank_up[...])

    ext[0:8, :] = edge[...].astype(F32)
    ext[8:, 0:DK] = pre_q[...].astype(F32)
    ext[8:, DK : 2 * DK] = pre_k[...].astype(F32)
    ext[8:, 2 * DK :] = pre_v[...].astype(F32)
    du_ext[n:, :] = jnp.zeros((8, du_ext.shape[1]), F32)
    du_ext[0:n, 0:DK] = dq * (DK**-0.5) * (sq * (1.0 + uq * (1.0 - sq)))
    du_ext[0:n, DK : 2 * DK] = dk * (sk * (1.0 + uk * (1.0 - sk)))
    dv = contract_rows(scores[...], dm) + dot(closing, later_b)
    for half in range(2):
        uv = u_in[:, (2 + half) * DK : (3 + half) * DK]
        sv = jax.nn.sigmoid(uv)
        du_ext[0:n, (2 + half) * DK : (3 + half) * DK] = dv[:, half * DK : (half + 1) * DK] * (
            sv * (1.0 + uv * (1.0 - sv))
        )
    ahead = []
    for back in range(1, TAPS):
        mask_row = jnp.sum(jnp.where(rows == cols, masks[back - 1], 0.0), axis=0, keepdims=True)
        ahead.append(column(mask_row, rows, cols, -back))
    for part in range(4):
        lanes = slice(part * DK, (part + 1) * DK)
        du = du_ext[0:n, lanes]
        d_pre = du * taps[3:4, lanes]
        back_rows = jnp.zeros((8, DK), F32)
        taps_out[3:4, lanes] = jnp.sum(du * ext[8 : 8 + n, lanes], axis=0, keepdims=True)
        for back in range(1, TAPS):
            weight = taps[3 - back : 4 - back, lanes]
            d_pre = d_pre + du_ext[back : back + n, lanes] * weight * ahead[back - 1]
            masked = du * masks[back - 1]
            taps_out[3 - back : 4 - back, lanes] = jnp.sum(
                masked * ext[8 - back : 8 - back + n, lanes], axis=0, keepdims=True
            )
            small[0:8, :] = jnp.zeros((8, DK), F32)
            small[8:16, :] = masked[0:8]
            back_rows = back_rows + small[back : back + 8, :] * weight
        back_rows_out[:, lanes] = back_rows
        last_rows_out[:, lanes] = d_pre[n - 8 :]
        rounded = d_pre.astype(BF16)
        for b in range(blocks):
            at = pl.multiple_of((m ^ b) * BLOCK, BLOCK)
            d_pre_out[pl.ds(at, BLOCK), lanes] = rounded[b * BLOCK : (b + 1) * BLOCK]


def call(body, outs, scratch, args, flops, placed=True):
    in_specs = [pl.BlockSpec(memory_space=pltpu.VMEM) for _ in args]
    if placed:
        in_specs[0] = pl.BlockSpec(memory_space=pltpu.SMEM)
    moved = sum(a.size * a.dtype.itemsize for a in args)
    return pl.pallas_call(
        body,
        out_shape=[jax.ShapeDtypeStruct(shape, kind) for shape, kind in outs],
        in_specs=in_specs,
        out_specs=[pl.BlockSpec(memory_space=pltpu.VMEM) for _ in outs],
        scratch_shapes=[pltpu.VMEM(shape, kind) for shape, kind in scratch],
        compiler_params=pltpu.CompilerParams(vmem_limit_bytes=VMEM_LIMIT),
        cost_estimate=pl.CostEstimate(flops=flops, bytes_accessed=moved, transcendentals=0),
    )(*args)


def on_device(
    block_input,
    first_gain,
    query_weight,
    key_weight,
    value_weight,
    query_conv,
    key_conv,
    value_conv,
    lowrank_down,
    lowrank_up,
    decay_bias,
    outgate_weight,
    outnorm_gain,
    output_weight,
    second_gain,
    gate_weight,
    up_weight,
    down_weight,
    starts,
    valid_mask,
    cotangent,
    teacher,
):
    length = block_input.shape[0]
    quarter, half = length // 4, length // 2
    places = lax.axis_size("seq")
    turns = places // 2
    share = D // places
    seq, head = lax.axis_index("seq"), lax.axis_index("head")
    mine = (head % 2) * 2 + head // 2
    zone, side = seq // 2, seq % 2
    place = mine.astype(jnp.int32).reshape(1)
    loss_weight = float(length * places * D // 8)

    def own(x):
        return lax.dynamic_slice_in_dim(x, mine * quarter, quarter, 0)

    def own_first(x):
        return jnp.concatenate(
            [lax.dynamic_slice_in_dim(x, (mine ^ p) * quarter, quarter, 0) for p in range(4)], axis=0
        )

    def natural(own_rows):
        near = gather_half(own_rows)
        swapped = jnp.concatenate([near[quarter:], near[:quarter]], axis=0)
        near = jnp.where(head // 2 == 0, near, swapped)
        far = flip(near, "head", 1)
        return jnp.where(
            head % 2 == 0,
            jnp.concatenate([near, far], axis=0),
            jnp.concatenate([far, near], axis=0),
        ).astype(F32)

    def rows_of(x, where):
        return lax.dynamic_slice_in_dim(x, where * share, share, 1)

    valid_float = valid_mask.astype(F32)
    valid_count = total(jnp.full((8, 128), jnp.sum(valid_float), F32), ["seq"])[0, 0]
    input_float = block_input.astype(F32)
    normed = (input_float * root_scale(input_float) * first_gain).astype(BF16)
    pre_k = dot(normed, key_weight).astype(BF16)
    pre_v = dot(normed, value_weight).astype(BF16)
    pre_q = dot(normed, query_weight).astype(BF16)
    start_row = starts.astype(F32).reshape(1, length)
    last_start, before_last = start_row[0, length - 1], start_row[0, length - 2]
    keep_one = 1.0 - last_start
    tail_keep = jnp.concatenate(
        [jnp.zeros((5,), F32), jnp.stack([keep_one * (1.0 - before_last), keep_one, jnp.ones((), F32)])]
    )
    tails = jnp.concatenate([pre_q[length - 8 :], pre_k[length - 8 :], pre_v[length - 8 :]], axis=1)
    edge = shift(tails * tail_keep[:, None].astype(BF16), "seq", 1)
    taps = jnp.concatenate([query_conv, key_conv, value_conv], axis=1)
    low_rank = dot(normed, lowrank_down).astype(BF16)
    bias_row = decay_bias.reshape(1, DK)
    channels = 2 * DK + DV
    u, v, x, logit, end_state, last = call(
        state_kernel,
        [
            ((length, channels), F32),
            ((length, DV), BF16),
            ((length, DK), F32),
            ((length, DK), F32),
            ((DK, DV), F32),
            ((1, DK), F32),
        ],
        [((length + 8, channels), F32)],
        (pre_q, pre_k, pre_v, edge, taps, start_row, low_rank, lowrank_up, bias_row),
        400_000_000,
        placed=False,
    )
    outgate = dot(normed, outgate_weight)
    last = last.reshape(DK)
    state_in = carry(last, end_state, 1).astype(BF16)
    gain_row = outnorm_gain.reshape(1, DV)
    gated, mixed, scores = call(
        output_kernel,
        [((length, DV), BF16), ((length, DV), F32), ((length, length), BF16)],
        [],
        (place, u, v, x, start_row, state_in, outgate, gain_row),
        400_000_000,
    )

    def parts(make):
        far = make(slice(half, length))
        return make(slice(0, half)), far

    branch = scatter_sum(parts(lambda r: contract_cols(gated[r], output_weight)))
    input_own = own(block_input).astype(F32)
    hidden = input_own + branch
    second_scale = root_scale(hidden)
    ffn_half = gather_half((hidden * second_scale * second_gain).astype(BF16))
    ffn_in = gather_full(ffn_half)
    gate_val = dot(ffn_in, gate_weight)
    up_val = dot(ffn_in, up_weight)
    sigmoid_gate = jax.nn.sigmoid(gate_val)
    activated = (gate_val * sigmoid_gate * up_val).astype(BF16)
    ffn_out = scatter_sum(parts(lambda r: contract_cols(activated[r], down_weight)))
    output_own = hidden + ffn_out
    valid_own = own(valid_float)[:, None]
    mismatch = output_own - own(teacher).astype(F32)
    squared = jnp.sum(valid_own * mismatch * mismatch)
    d_out = own(cotangent).astype(F32) + valid_own * 2.0 * loss_weight * mismatch / (valid_count * D)
    d_ffn_half = gather_half(d_out.astype(BF16))
    d_ffn = gather_full(d_ffn_half)
    d_act = dot(d_ffn, down_weight)
    d_gate_val = (d_act * up_val * sigmoid_gate * (1.0 + gate_val * (1.0 - sigmoid_gate))).astype(BF16)
    d_up_val = (d_act * gate_val * sigmoid_gate).astype(BF16)
    d_nffn = scatter_sum(
        parts(
            lambda r: contract_cols(d_gate_val[r], gate_weight) + contract_cols(d_up_val[r], up_weight)
        )
    )
    second_part = jnp.sum(d_nffn * hidden * second_scale, axis=0)
    d_hidden = d_out + norm_backward(hidden, second_scale, second_gain, d_nffn)
    d_branch_half = gather_half(d_hidden.astype(BF16))
    d_branch = gather_full(d_branch_half)

    d_gated = dot(d_branch, output_weight)
    d_outgate, d_mixed, outnorm_part, direct = call(
        gate_back_kernel,
        [((length, DV), BF16), ((length, DV), BF16), ((1, DV), F32), ((DK, DV), F32)],
        [((length, DV), F32)],
        (place, d_gated, mixed, outgate, gain_row, u[:, :DK], x, start_row),
        200_000_000,
    )
    later = carry(last, direct, -1)
    d_pre, last_rows, back_rows, taps_part, d_low, lowup_part, bias_part = call(
        mixer_back_kernel,
        [
            ((length, channels), BF16),
            ((8, channels), F32),
            ((8, channels), F32),
            ((TAPS, channels), F32),
            ((length, RANK), F32),
            ((RANK, DK), F32),
            ((1, DK), F32),
        ],
        [
            ((length + 8, channels), F32),
            ((length + 8, channels), F32),
            ((16, DK), F32),
            ((length, DK), F32),
        ],
        (
            place, d_mixed, state_in, later, u, v, x, scores, pre_q, pre_k, pre_v, edge, taps,
            logit, start_row, low_rank, lowrank_up,
        ),
        1_000_000_000,
    )
    from_next = shift(back_rows, "seq", -1)
    fixed = (last_rows + from_next * tail_keep[:, None]).astype(BF16)
    d_pre = lax.dynamic_update_slice(d_pre, fixed, ((mine ^ 3) * quarter + quarter - 8, 0))
    d_lowrank = total(d_low, ["head"]).astype(BF16)
    d_first = scatter_sum(
        parts(
            lambda r: contract_cols(d_outgate[r], outgate_weight)
            + contract_cols(d_pre[r, :DK], query_weight)
            + contract_cols(d_pre[r, DK : 2 * DK], key_weight)
            + contract_cols(d_pre[r, 2 * DK :], value_weight)
        )
    )
    d_first = d_first + contract_cols(own(d_lowrank), lowrank_down)
    first_scale = root_scale(input_own)
    first_part = jnp.sum(d_first * input_own * first_scale, axis=0)
    grad_own = d_hidden + norm_backward(input_own, first_scale, first_gain, d_first)
    block_output = natural(output_own.astype(BF16))
    grad_input = natural(grad_own.astype(BF16))

    def collect(half_rows):
        got = ring(half_rows)
        return jnp.concatenate(got + [flip(g, "head", 1) for g in got], axis=0)

    ffn_far, d_ffn_far = collect(ffn_half), collect(d_ffn_half)
    gate_far, up_far = dot(ffn_far, gate_weight), dot(ffn_far, up_weight)
    act_far = dot(d_ffn_far, down_weight)
    sig_far = jax.nn.sigmoid(gate_far)
    activated_far = (gate_far * sig_far * up_far).astype(BF16)
    d_gate_far = (act_far * up_far * sig_far * (1.0 + gate_far * (1.0 - sig_far))).astype(BF16)
    d_up_far = (act_far * gate_far * sig_far).astype(BF16)

    def pair_sum(make):
        sent = make(zone * 2 + 1 - side).astype(BF16)
        got = flip(sent, "seq", 1)
        return make(zone * 2 + side) + got.astype(F32)

    def ffn_grad(near_left, far_left, near_right, far_right):
        return pair_sum(
            lambda where: contract_rows(rows_of(near_left, where), near_right)
            + contract_rows(rows_of(far_left, where), far_right)
        )

    grad_gate = ffn_grad(ffn_in, ffn_far, d_gate_val, d_gate_far)
    grad_up = ffn_grad(ffn_in, ffn_far, d_up_val, d_up_far)
    grad_down = ffn_grad(d_ffn, d_ffn_far, activated, activated_far)

    def slices(x, half_rows):
        both = [lax.dynamic_slice_in_dim(x, zone * 2 * share, 2 * share, 1)]
        for by in range(1, turns):
            target = lax.rem(zone + by, turns)
            sent = lax.dynamic_slice_in_dim(half_rows, target * 2 * share, 2 * share, 1)
            got = turn(sent, by)
            both.append(jnp.concatenate([got, flip(got, "head", 1)], axis=0))
        return both

    def mixer_grad(lefts, right):
        rights = [right, *ring(right)]

        def make(where):
            at = (where - zone * 2) * share
            acc = None
            for left, one in zip(lefts, rights):
                term = contract_rows(lax.dynamic_slice_in_dim(left, at, share, 1), one)
                acc = term if acc is None else acc + term
            return acc

        return pair_sum(make)

    normed_first = own_first(normed)
    normed_slices = slices(normed_first, normed_first[:half])
    branch_slices = slices(d_branch, d_branch_half)
    grad_output = mixer_grad(branch_slices, gated)
    grad_outgate = mixer_grad(normed_slices, d_outgate)
    grad_pre = mixer_grad(normed_slices, d_pre)

    shared = jnp.concatenate(
        [second_part.reshape(4, DV), outnorm_part, jnp.full((3, DV), squared, F32)], axis=0
    )
    shared = total(shared, ["seq", "head"])
    grad_second_gain = shared[0:4].reshape(D)
    grad_outnorm = shared[4]
    distill = shared[5, 0] / (valid_count * D)
    first_total = total(first_part.reshape(4, DV), ["seq", "head"]).reshape(D)
    low_part = contract_rows(d_lowrank, normed)
    apart = jnp.concatenate(
        [
            taps_part.reshape(2, D),
            lowup_part.reshape(2, D),
            jnp.concatenate([bias_part, jnp.zeros((1, D - DK), F32)], axis=1),
            jnp.zeros((3, D), F32),
            low_part,
        ],
        axis=0,
    )
    apart = total(apart, ["seq"])
    taps_sum = apart[0:2].reshape(TAPS, channels)
    grad_lowrank_up = apart[2:4].reshape(RANK, DK)
    grad_bias = apart[4, :DK]
    grad_lowrank_down = lax.dynamic_slice_in_dim(apart[8:], seq * share, share, 1).T
    return (
        block_output,
        distill,
        grad_input,
        first_total,
        grad_pre[:, :DK],
        grad_pre[:, DK : 2 * DK],
        grad_pre[:, 2 * DK :],
        taps_sum[:, :DK],
        taps_sum[:, DK : 2 * DK],
        taps_sum[:, 2 * DK :],
        grad_lowrank_down,
        grad_lowrank_up,
        grad_bias,
        grad_outgate,
        grad_outnorm,
        grad_output,
        grad_second_gain,
        grad_gate,
        grad_up,
        grad_down,
    )


def solution(mesh):
    rows, cols, whole = P("seq", None), P(None, "head"), P()
    in_specs = (
        rows, whole, cols, cols, cols, cols, cols, cols, whole, cols, P("head"), cols, whole, cols,
        whole, cols, cols, cols, P("seq"), P("seq"), rows, rows,
    )
    tiles = P("seq", "head")
    out_specs = (
        rows, whole, rows, whole, tiles, tiles, tiles, cols, cols, cols, rows, cols, P("head"), tiles,
        whole, tiles, whole, tiles, tiles, tiles,
    )
    return jax.shard_map(
        on_device, mesh=mesh, in_specs=in_specs, out_specs=out_specs, check_vma=False
    )
```

```python
import functools

import functools

import jax
import jax.numpy as jnp
from jax import lax
from jax.experimental import pallas as pl
from jax.experimental.pallas import tpu as pltpu
from jax.sharding import PartitionSpec as P

D = 2048
DK = 256
DV = 512
RANK = 16
TAPS = 4
BLOCK = 64
EPSILON = 1e-05
HIGHEST = lax.Precision.HIGHEST
F32 = jnp.float32
BF16 = jnp.bfloat16
MIB = 1024 * 1024


def contract_rows(left, right):
    return lax.dot_general(left, right, (((0,), (0,)), ((), ())), preferred_element_type=F32)


def contract_cols(left, right):
    return lax.dot_general(left, right, (((1,), (1,)), ((), ())), preferred_element_type=F32)


def dot(left, right, precision=None):
    return lax.dot_general(
        left, right, (((1,), (0,)), ((), ())), precision=precision, preferred_element_type=F32
    )


def root_scale(v):
    return lax.rsqrt(jnp.mean(v * v, axis=-1, keepdims=True) + EPSILON)


def norm_backward(v, scale, gain, upstream):
    scaled_up = upstream * gain
    return scale * scaled_up - v * scale * scale * scale * jnp.mean(
        scaled_up * v, axis=-1, keepdims=True
    )


def flip(x, axis, bit):
    n = lax.axis_size(axis)
    return lax.ppermute(x, axis, [(i, i ^ bit) for i in range(n)])


def shift(x, axis, by):
    n = lax.axis_size(axis)
    return lax.ppermute(x, axis, [(i, i + by) for i in range(n) if 0 <= i + by < n])


def turn(x, by):
    n = lax.axis_size("seq")
    return lax.ppermute(x, "seq", [(i, (i + 2 * by) % n) for i in range(n)])


def after(x, *others):
    return lax.optimization_barrier((x, *others))[0]


def join(*xs):
    return lax.optimization_barrier(xs)


def total(x, steps, kind=F32):
    for axis, bit in steps:
        if kind != F32:
            x = lax.reduce_precision(x, 8, 7)
        x = x + flip(x.astype(kind), axis, bit).astype(F32)
    return x


def grids(n):
    return (
        lax.broadcasted_iota(jnp.int32, (n, n), 0),
        lax.broadcasted_iota(jnp.int32, (n, n), 1),
    )


def column(row, rows, cols, back):
    return jnp.sum(jnp.where(cols == rows - back, row, 0.0), axis=1, keepdims=True)


def tap_masks(start_row, rows, cols):
    here, one, two = (column(start_row, rows, cols, back) for back in range(3))
    first = 1.0 - here
    second = first * (1.0 - one)
    return here, (first, second, second * (1.0 - two))


def segments(start_row, start_col, rows, cols):
    seg_col = jnp.sum(jnp.where(cols <= rows, start_row, 0.0), axis=1, keepdims=True)
    seg_row = jnp.sum(jnp.where(rows <= cols, start_col, 0.0), axis=0, keepdims=True)
    return seg_col, seg_row, jnp.sum(start_row)


def block_middles(x):
    n = x.shape[0] // BLOCK
    mids = []
    for b in range(n):
        last = x[(b + 1) * BLOCK - 1 : (b + 1) * BLOCK]
        before = x[b * BLOCK - 1 : b * BLOCK] if b else jnp.zeros_like(last)
        mids.append(0.5 * (before + last))
    return mids


def spread(mids):
    return jnp.concatenate(
        [jnp.broadcast_to(mid, (BLOCK, mid.shape[1])) for mid in mids], axis=0
    )


def state_kernel(
    place, pre_q, pre_k, pre_v, edge, taps, start_row, low_rank, lowrank_up, bias,
    u_out, v_out, x_out, logit_out, state_out, ext,
):
    n = pre_q.shape[0]
    rows, cols = grids(n)
    sr = start_row[...]
    start_col, masks = tap_masks(sr, rows, cols)
    seg_col, _, seg_last = segments(sr, start_col, rows, cols)
    ext[0:8, :] = edge[...].astype(F32)
    ext[8:, 0:DK] = pre_q[...].astype(F32)
    ext[8:, DK : 2 * DK] = pre_k[...].astype(F32)
    ext[8:, 2 * DK :] = pre_v[...].astype(F32)
    for part in range(4):
        lanes = slice(part * DK, (part + 1) * DK)
        u = ext[8 : 8 + n, lanes] * taps[3:4, lanes]
        for back in range(1, TAPS):
            u = u + ext[8 - back : 8 - back + n, lanes] * taps[3 - back : 4 - back, lanes] * masks[
                back - 1
            ]
        u_out[:, lanes] = u
        if part >= 2:
            v_out[:, (part - 2) * DK : (part - 1) * DK] = (u * jax.nn.sigmoid(u)).astype(BF16)
    logit = dot(low_rank[...], lowrank_up[...]) + bias[...]
    logit_out[...] = logit
    decays = (jnp.minimum(logit, 0.0) - jnp.log1p(jnp.exp(-jnp.abs(logit)))) * (1.0 / 16.0)
    x = dot((cols <= rows).astype(F32), decays, HIGHEST)
    x_out[...] = x
    u = u_out[:, DK : 2 * DK]
    keys = u * jax.nn.sigmoid(u)
    tail = (seg_col == seg_last).astype(F32)
    final = x[n - 1 : n]
    closing = (keys * jnp.exp(final - x) * tail).astype(BF16)
    put_decay(
        state_out,
        contract_rows(closing, v_out[...]).astype(BF16),
        jnp.exp(final) * (seg_last == 0.0).astype(F32),
    )


def local_scores(q, k, x):
    n = x.shape[0] // BLOCK
    mids = block_middles(x)
    mid = spread(mids)
    grow, shrink = jnp.exp(x - mid), jnp.exp(mid - x)
    rising, falling = q * grow, (k * shrink).astype(BF16)
    lifted, scales = [], []
    for j in range(n):
        pieces = [jnp.exp(mids[i] - mids[j]) for i in range(j, n)]
        scale = spread(pieces)
        scales.append(scale)
        lifted.append((rising[j * BLOCK :] * scale).astype(BF16))
    return grow, shrink, lifted, scales, falling


def output_kernel(
    place, u_qk, v, x_in, start_row, state_in, outgate, gain, weight,
    gated_out, mixed_out, scores_out, sent_out, kept_out,
):
    n = x_in.shape[0]
    blocks = n // BLOCK
    rows, cols = grids(n)
    sr = start_row[...]
    start_col = column(sr, rows, cols, 0)
    seg_col, seg_row, _ = segments(sr, start_col, rows, cols)
    allowed = (cols <= rows) & (seg_col == seg_row)
    alive = (seg_col == 0.0).astype(F32)
    x = x_in[...]
    uq = u_qk[:, 0:DK]
    uk = u_qk[:, DK : 2 * DK]
    q = uq * jax.nn.sigmoid(uq) * DK**-0.5
    k = uk * jax.nn.sigmoid(uk)
    _, _, lifted, _, falling = local_scores(q, k, x)
    scores_out[...] = jnp.zeros_like(scores_out)
    for j in range(blocks):
        lo, hi = j * BLOCK, (j + 1) * BLOCK
        s = contract_cols(lifted[j], falling[lo:hi])
        scores_out[lo:, lo:hi] = jnp.where(allowed[lo:, lo:hi], s, 0.0).astype(BF16)
    carried = (q * jnp.exp(x) * alive).astype(BF16)
    out = dot(scores_out[...], v[...]) + dot(carried, state_in[...])
    mixed_out[...] = out
    og = outgate[...]
    gated = (out * root_scale(out) * gain[...] * (og * jax.nn.sigmoid(og))).astype(BF16)
    m = place[0]
    for b in range(blocks):
        at = pl.multiple_of((m ^ b) * BLOCK, BLOCK)
        gated_out[pl.ds(at, BLOCK), :] = gated[b * BLOCK : (b + 1) * BLOCK]
    half = n // 2
    for part in range(4):
        lanes = slice(part * DV, (part + 1) * DV)
        branch = contract_cols(gated_out[...], weight[lanes, :])
        kept_out[:, lanes] = branch[0:half]
        sent_out[:, lanes] = branch[half:].astype(BF16)


def gate_back_kernel(
    place, branch_0, branch_1, branch_2, branch_3, weight, mixed, outgate, gain, u_in, x_in,
    start_row, d_outgate_out, d_mixed_out, gain_out, direct_out, cut_out, order,
):
    n = x_in.shape[0]
    blocks = n // BLOCK
    m = place[0]
    for p, piece in enumerate((branch_0, branch_1, branch_2, branch_3)):
        at = pl.multiple_of((m ^ p) * BLOCK, BLOCK)
        order[pl.ds(at, BLOCK), :] = piece[...]
        cut_out[p * BLOCK : (p + 1) * BLOCK, :] = piece[:, pair_lanes(place, cut_out)]
    up = dot(order[...], weight[...])
    og = outgate[...]
    sig = jax.nn.sigmoid(og)
    out = mixed[...]
    scale = root_scale(out)
    g = gain[...]
    d_outgate = (up * (out * scale * g) * sig * (1.0 + og * (1.0 - sig))).astype(BF16)
    for b in range(blocks):
        at = pl.multiple_of((m ^ b) * BLOCK, BLOCK)
        d_outgate_out[pl.ds(at, BLOCK), :] = d_outgate[b * BLOCK : (b + 1) * BLOCK]
    d_norm = up * (og * sig)
    gain_out[...] = jnp.sum(d_norm * out * scale, axis=0, keepdims=True)
    d_mixed = norm_backward(out, scale, g, d_norm).astype(BF16)
    d_mixed_out[...] = d_mixed
    rows, cols = grids(n)
    sr = start_row[...]
    seg_col = jnp.sum(jnp.where(cols <= rows, sr, 0.0), axis=1, keepdims=True)
    alive = (seg_col == 0.0).astype(F32)
    uq = u_in[:, 0:DK]
    x = x_in[...]
    carried = (uq * jax.nn.sigmoid(uq) * DK**-0.5 * jnp.exp(x) * alive).astype(BF16)
    put_decay(
        direct_out,
        contract_rows(carried, d_mixed).astype(BF16),
        jnp.exp(x[n - 1 : n]) * (jnp.sum(sr) == 0.0).astype(F32),
    )


def mixer_back_kernel(
    place, d_mixed, state_in, later, u_in, v, x_in, scores, pre_q, pre_k, pre_v, edge, taps,
    logit, start_row, low_rank, lowrank_up,
    d_pre_out, last_rows_out, pack_out, d_low_out, back_rows_out,
    ext, du_ext, small, dx_buf,
):
    n = x_in.shape[0]
    blocks = n // BLOCK
    m = place[0]
    rows, cols = grids(n)
    sr = start_row[...]
    start_col, masks = tap_masks(sr, rows, cols)
    seg_col, seg_row, seg_last = segments(sr, start_col, rows, cols)
    allowed = (cols <= rows) & (seg_col == seg_row)
    alive = (seg_col == 0.0).astype(F32)
    tail = (seg_col == seg_last).astype(F32)
    x = x_in[...]
    uq = u_in[:, 0:DK]
    uk = u_in[:, DK : 2 * DK]
    sq, sk = jax.nn.sigmoid(uq), jax.nn.sigmoid(uk)
    q = uq * sq * DK**-0.5
    k = uk * sk
    grow, shrink, lifted, scales, falling = local_scores(q, k, x)
    dm = d_mixed[...]
    later_b = later[...]
    later_f = later_b.astype(F32)
    state_f = state_in[...].astype(F32)
    d_scores = jnp.where(allowed, contract_cols(dm, v[...]), 0.0).astype(BF16)
    final = x[n - 1 : n]
    leaving = jnp.exp(final - x) * tail
    closing = (k * leaving).astype(BF16)
    d_closing = contract_cols(v[...], later_b)
    entering = jnp.exp(x) * alive
    d_carried = contract_cols(dm, state_in[...])
    dq = d_carried * entering
    dk = d_closing * leaving
    closed = d_closing * closing.astype(F32)
    dx_buf[...] = d_carried * (q * entering) - closed
    through = jnp.sum(later_f * state_f, axis=1, keepdims=True)
    through_row = jnp.sum(jnp.where(rows == cols, through, 0.0), axis=0, keepdims=True)
    at_last = jnp.sum(closed, axis=0, keepdims=True) + through_row * jnp.exp(final) * (
        seg_last == 0.0
    ).astype(F32)
    dx_buf[n - 1 : n, :] = dx_buf[n - 1 : n, :] + at_last
    dq_parts = [dq[b * BLOCK : (b + 1) * BLOCK] for b in range(blocks)]
    dk_parts = []
    for j in range(blocks):
        lo, hi = j * BLOCK, (j + 1) * BLOCK
        ds = d_scores[lo:, lo:hi]
        d_lift = dot(ds, falling[lo:hi])
        d_fall = contract_rows(ds, lifted[j])
        dx_buf[lo:, :] = dx_buf[lo:, :] + d_lift * lifted[j].astype(F32)
        dx_buf[lo:hi, :] = dx_buf[lo:hi, :] - d_fall * falling[lo:hi].astype(F32)
        d_rise = d_lift * scales[j] * grow[lo:]
        for b in range(j, blocks):
            dq_parts[b] = dq_parts[b] + d_rise[(b - j) * BLOCK : (b - j + 1) * BLOCK]
        dk_parts.append(dk[lo:hi] + d_fall * shrink[lo:hi])
    dq = jnp.concatenate(dq_parts, axis=0)
    dk = jnp.concatenate(dk_parts, axis=0)
    d_decays = dot((cols >= rows).astype(F32), dx_buf[...], HIGHEST)
    d_logit = (d_decays * jax.nn.sigmoid(-logit[...]) * (1.0 / 16.0)).astype(BF16)
    pack_out[...] = jnp.zeros_like(pack_out)
    pack_out[4:5, 0:DK] = jnp.sum(d_logit.astype(F32), axis=0, keepdims=True)
    d_up = contract_rows(low_rank[...], d_logit)
    per = pack_out.shape[1] // DK
    for row in range(RANK):
        at = (row % per) * DK
        pack_out[2 + row // per : 3 + row // per, at : at + DK] = d_up[row : row + 1]
    d_low_out[...] = contract_cols(lowrank_up[...], d_logit)

    ext[0:8, :] = edge[...].astype(F32)
    ext[8:, 0:DK] = pre_q[...].astype(F32)
    ext[8:, DK : 2 * DK] = pre_k[...].astype(F32)
    ext[8:, 2 * DK :] = pre_v[...].astype(F32)
    du_ext[n:, :] = jnp.zeros((8, du_ext.shape[1]), F32)
    du_ext[0:n, 0:DK] = dq * (DK**-0.5) * (sq * (1.0 + uq * (1.0 - sq)))
    du_ext[0:n, DK : 2 * DK] = dk * (sk * (1.0 + uk * (1.0 - sk)))
    dv = contract_rows(scores[...], dm) + dot(closing, later_b)
    for half in range(2):
        uv = u_in[:, (2 + half) * DK : (3 + half) * DK]
        sv = jax.nn.sigmoid(uv)
        du_ext[0:n, (2 + half) * DK : (3 + half) * DK] = dv[:, half * DK : (half + 1) * DK] * (
            sv * (1.0 + uv * (1.0 - sv))
        )
    ahead = []
    for back in range(1, TAPS):
        mask_row = jnp.sum(jnp.where(rows == cols, masks[back - 1], 0.0), axis=0, keepdims=True)
        ahead.append(column(mask_row, rows, cols, -back))
    for part in range(4):
        lanes = slice(part * DK, (part + 1) * DK)
        du = du_ext[0:n, lanes]
        d_pre = du * taps[3:4, lanes]
        back_rows = jnp.zeros((8, DK), F32)
        wide = du_ext.shape[1]
        pack_out[1:2, wide + part * DK : wide + (part + 1) * DK] = jnp.sum(
            du * ext[8 : 8 + n, lanes], axis=0, keepdims=True
        )
        for back in range(1, TAPS):
            weight = taps[3 - back : 4 - back, lanes]
            d_pre = d_pre + du_ext[back : back + n, lanes] * weight * ahead[back - 1]
            masked = du * masks[back - 1]
            row, at = (3 - back) // 2, (3 - back) % 2 * wide + part * DK
            pack_out[row : row + 1, at : at + DK] = jnp.sum(
                masked * ext[8 - back : 8 - back + n, lanes], axis=0, keepdims=True
            )
            small[0:8, :] = jnp.zeros((8, DK), F32)
            small[8:16, :] = masked[0:8]
            back_rows = back_rows + small[back : back + 8, :] * weight
        back_rows_out[:, lanes] = back_rows
        last_rows_out[:, lanes] = d_pre[n - 8 :]
        rounded = d_pre.astype(BF16)
        for b in range(blocks):
            at = pl.multiple_of((m ^ b) * BLOCK, BLOCK)
            d_pre_out[pl.ds(at, BLOCK), lanes] = rounded[b * BLOCK : (b + 1) * BLOCK]


def whole_spec():
    return pl.BlockSpec(memory_space=pltpu.VMEM)


def call(body, place, args, outs, scratch=(), vmem=6, micros=1.0):
    return pl.pallas_call(
        body,
        out_shape=[jax.ShapeDtypeStruct(shape, kind) for shape, kind in outs],
        in_specs=[pl.BlockSpec(memory_space=pltpu.SMEM)] + [whole_spec() for _ in args],
        out_specs=[whole_spec() for _ in outs],
        scratch_shapes=[pltpu.VMEM(shape, kind) for shape, kind in scratch],
        compiler_params=pltpu.CompilerParams(vmem_limit_bytes=vmem * MIB),
        cost_estimate=pl.CostEstimate(
            flops=int(micros * 1e9), bytes_accessed=int(micros * 3e6), transcendentals=0
        ),
    )(place, *args)


def spans(width, tile):
    return [slice(at, min(at + tile, width)) for at in range(0, width, tile)]


def fold_kernel(place, kept, got, near_out, far_out):
    quarter = near_out.shape[0]
    near_out[...] = kept[0:quarter] + got[0:quarter].astype(F32)
    far_out[...] = (kept[quarter:] + got[quarter:].astype(F32)).astype(BF16)


def hidden_kernel(place, kept, got, own_input, gain, hidden_out, ffn_out):
    hidden = own_input[...].astype(F32) + (kept[...] + got[...].astype(F32))
    hidden_out[...] = hidden
    ffn_out[...] = (hidden * root_scale(hidden) * gain[...]).astype(BF16)


def loss_kernel(
    weight, place, kept, got, hidden, teacher, cotangent, valid, count,
    output_out, d_out_out, d_ffn_out, squared_out,
):
    output = hidden[...] + (kept[...] + got[...].astype(F32))
    output_out[...] = output.astype(BF16)
    mismatch = output - teacher[...].astype(F32)
    keep = valid[...]
    squares = jnp.sum(keep * mismatch * mismatch, axis=0, keepdims=True)
    squared_out[...] = jnp.sum(squares, axis=1, keepdims=True)
    d_out = cotangent[...].astype(F32) + keep * (2.0 * weight) * mismatch / (count[...] * D)
    d_out_out[...] = d_out
    d_ffn_out[...] = d_out.astype(BF16)


def hidden_back_kernel(
    place, kept, got, hidden, d_out, gain, d_hidden_out, d_branch_out, gain_out
):
    d_norm = kept[...] + got[...].astype(F32)
    h = hidden[...]
    scale = root_scale(h)
    gain_out[...] = jnp.sum(d_norm * h * scale, axis=0, keepdims=True)
    d_hidden = d_out[...] + norm_backward(h, scale, gain[...], d_norm)
    d_hidden_out[...] = d_hidden
    d_branch_out[...] = d_hidden.astype(BF16)


def input_back_kernel(
    place, kept, got, own_input, d_hidden, gain, d_low, down_turned, grad_out, gain_out
):
    d_norm = (kept[...] + got[...].astype(F32)) + contract_rows(d_low[...], down_turned[...])
    v = own_input[...].astype(F32)
    scale = root_scale(v)
    gain_out[...] = jnp.sum(d_norm * v * scale, axis=0, keepdims=True)
    grad_out[...] = (d_hidden[...] + norm_backward(v, scale, gain[...], d_norm)).astype(BF16)


def carry_kernel(first, last, place, got, *refs):
    refs = list(refs)
    window = None if last else refs.pop(0)
    found = None if first else refs.pop(0)
    n = DK
    rows, cols = grids(n)

    def as_column(row):
        return jnp.sum(jnp.where(rows == cols, row, 0.0), axis=1, keepdims=True)

    def decay_of(ref):
        both = ref[n : n + 1, :].astype(F32)
        return both[:, 0:n] + both[:, n : 2 * n]

    arrived = got[0:n, :].astype(F32)
    if first:
        merged = arrived
        found_decay = decay_of(got)
    else:
        own = decay_of(found)
        merged = as_column(own) * arrived + found[0:n, :].astype(F32)
        found_decay = own * decay_of(got)
    if last:
        refs.pop(0)[...] = merged.astype(BF16)
        return
    window_decay = decay_of(window)
    state = as_column(window_decay) * arrived + window[0:n, :].astype(F32)
    put_decay(refs.pop(0), state.astype(BF16), window_decay * decay_of(got))
    put_decay(refs.pop(0), merged.astype(BF16), found_decay)


def put_decay(ref, state, decay):
    n = DK
    ref[0:n, :] = state
    high = decay.astype(BF16)
    low = (decay - high.astype(F32)).astype(BF16)
    row = jnp.concatenate([high, low], axis=1)
    ref[n:, :] = jnp.broadcast_to(row, (ref.shape[0] - n, 2 * n))


def rows_kernel(count, widths, place, *refs):
    lefts, rights = refs[:count], refs[count : count + len(widths)]
    sent, kept = refs[count + len(widths) :]
    half = sent.shape[0]
    for lanes in spans(kept.shape[1], 1024):
        acc = None
        for (left, at, width), right in zip(widths, rights):
            term = contract_cols(lefts[left][:, at : at + width], right[lanes, :])
            acc = term if acc is None else acc + term
        kept[:, lanes] = acc[0:half]
        sent[:, lanes] = acc[half:].astype(BF16)


def rows_times(lefts, pairs):
    half = lefts[0].shape[0] // 2
    widths = [pair[:3] for pair in pairs]
    return (
        functools.partial(rows_kernel, len(lefts), widths),
        [*lefts, *(pair[3] for pair in pairs)],
        [((half, D), BF16), ((half, D), F32)],
    )


def stack(pieces, buf):
    at = 0
    for piece in pieces:
        buf[at : at + piece.shape[0], :] = piece[...]
        at += piece.shape[0]


def pair_lanes(place, cut_out):
    pair = cut_out.shape[1]
    return pl.ds(pl.multiple_of(place[1] * pair, pair), pair)


def gate_kernel(count, place, *refs):
    pieces, (gate_w, up_w, act_out, gate_out, up_out, cut_out, buf) = refs[:count], refs[count:]
    stack(pieces, buf)
    cut_out[...] = buf[:, pair_lanes(place, cut_out)]
    for lanes in spans(act_out.shape[1], 256):
        gate, up = dot(buf[...], gate_w[:, lanes]), dot(buf[...], up_w[:, lanes])
        sig = jax.nn.sigmoid(gate)
        swish = gate * sig
        act_out[:, lanes] = (swish * up).astype(BF16)
        gate_out[:, lanes] = (up * sig * (1.0 + gate * (1.0 - sig))).astype(gate_out.dtype)
        up_out[:, lanes] = swish.astype(up_out.dtype)


def gate_up(pair, pieces, gate_weight, up_weight, kind):
    length = sum(p.shape[0] for p in pieces)
    width = gate_weight.shape[1]
    return (
        functools.partial(gate_kernel, len(pieces)),
        [*pieces, gate_weight, up_weight],
        [
            ((length, width), BF16),
            ((length, width), kind),
            ((length, width), kind),
            ((length, pair), BF16),
        ],
        [((length, D), BF16)],
    )


def gate_back_kernel_rows(count, place, *refs):
    pieces, (down_w, gate_in, up_in, d_gate_out, d_up_out, cut_out, buf) = refs[:count], refs[count:]
    stack(pieces, buf)
    cut_out[...] = buf[:, pair_lanes(place, cut_out)]
    for lanes in spans(d_gate_out.shape[1], 256):
        d_act = dot(buf[...], down_w[:, lanes])
        d_gate_out[:, lanes] = (d_act * gate_in[:, lanes].astype(F32)).astype(BF16)
        d_up_out[:, lanes] = (d_act * up_in[:, lanes].astype(F32)).astype(BF16)


def gate_back_rows(pair, pieces, down_weight, gate_in, up_in):
    length, width = gate_in.shape
    return (
        functools.partial(gate_back_kernel_rows, len(pieces)),
        [*pieces, down_weight, gate_in, up_in],
        [((length, width), BF16), ((length, width), BF16), ((length, pair), BF16)],
        [((length, D), BF16)],
    )


def weight_kernel(kind, blocks, place, *refs):
    sent, kept, left_buf, res = refs[-4:]
    rights, lefts = refs[-4 - blocks : -4], refs[: -4 - blocks]
    m, side = place[0], place[2]
    share = kept.shape[0]
    length = rights[0].shape[0]
    quarter = length // 4
    if kind == "cuts":
        stack(lefts, left_buf)
    else:
        if kind == "natural":
            lanes = pair_lanes(place, left_buf)
            for p in range(4):
                rows = pl.ds(pl.multiple_of((m ^ p) * quarter, quarter), quarter)
                left_buf[p * quarter : (p + 1) * quarter, :] = lefts[0][rows, lanes]
        else:
            left_buf[0:length, :] = lefts[0][...]
        for block in range(1, blocks):
            for p in range(4):
                at = block * length + p * quarter
                piece = lefts[1 + p][(block - 1) * quarter : block * quarter, :]
                left_buf[at : at + quarter, :] = piece
    for cols in spans(kept.shape[1], 256):
        acc = None
        for block, right in enumerate(rights):
            term = contract_rows(
                left_buf[block * length : (block + 1) * length, :], right[:, cols]
            )
            acc = term if acc is None else acc + term
        width = cols.stop - cols.start
        res[:, 0:width] = acc
        sent[:, cols] = res[
            pl.ds(pl.multiple_of((1 - side) * share, share), share), 0:width
        ].astype(BF16)
        kept[:, cols] = res[pl.ds(pl.multiple_of(side * share, share), share), 0:width]


def weight_args(kind, share, lefts, rights):
    tokens, width = rights[0].shape[0] * len(rights), rights[0].shape[1]
    return (
        functools.partial(weight_kernel, kind, len(rights)),
        [*lefts, *rights],
        [((share, width), BF16), ((share, width), F32)],
        [((tokens, 2 * share), BF16), ((2 * share, 256), F32)],
    )


def natural_kernel(place, piece_0, piece_1, piece_2, piece_3, out):
    quarter = piece_0.shape[0]
    for p, piece in enumerate((piece_0, piece_1, piece_2, piece_3)):
        at = pl.multiple_of((place[0] ^ p) * quarter, quarter)
        out[pl.ds(at, quarter), :] = piece[...].astype(F32)


def settle_kernel(place, kept, got, out_0, out_1, out_2):
    at = 0
    for out in (out_0, out_1, out_2):
        width = out.shape[1]
        out[...] = kept[:, at : at + width] + got[:, at : at + width].astype(F32)
        at += width


def low_kernel(place, d_low, normed, pack, out):
    out[0:RANK, :] = dot(d_low[...], normed[...])
    out[RANK:, :] = pack[...]


def unpack_kernel(share, place, summed, query_out, key_out, value_out, up_out, bias_out, down_out):
    for row in range(TAPS):
        at = (row % 2) * (2 * DK + DV)
        line = summed[RANK + row // 2 : RANK + 1 + row // 2, :]
        query_out[row : row + 1, :] = line[:, at : at + DK]
        key_out[row : row + 1, :] = line[:, at + DK : at + 2 * DK]
        value_out[row : row + 1, :] = line[:, at + 2 * DK : at + 2 * DK + DV]
    per = D // DK
    for row in range(RANK):
        at = (row % per) * DK
        up_out[row : row + 1, :] = summed[RANK + 2 + row // per : RANK + 3 + row // per, at : at + DK]
    bias_out[...] = summed[RANK + 4 : RANK + 5, 0:DK]
    pair = 2 * share
    both = summed[0:RANK, pl.ds(pl.multiple_of(place[1] * pair, pair), pair)]
    down_out[...] = jnp.where(place[2] == 0, both[:, 0:share], both[:, share:])


COST = {
    "state_kernel": 2.3,
    "output_kernel": 2.0,
    "gate_back_kernel": 2.0,
    "mixer_back_kernel": 4.5,
    "rows_kernel": 2.8,
    "gate_kernel": 4.0,
    "gate_back_kernel_rows": 2.4,
    "weight_kernel": 2.4,
    "natural_kernel": 2.0,
}


def on_device(
    block_input,
    first_gain,
    query_weight,
    key_weight,
    value_weight,
    query_conv,
    key_conv,
    value_conv,
    lowrank_down,
    lowrank_up,
    decay_bias,
    outgate_weight,
    outnorm_gain,
    output_weight,
    second_gain,
    gate_weight,
    up_weight,
    down_weight,
    starts,
    valid_mask,
    cotangent,
    teacher,
):
    length = block_input.shape[0]
    quarter, half = length // 4, length // 2
    places = lax.axis_size("seq")
    turns = places // 2
    share = D // places
    pair = 2 * share
    hidden_units = gate_weight.shape[1]
    channels = 2 * DK + DV
    seq, head = lax.axis_index("seq"), lax.axis_index("head")
    mine = (head % 2) * 2 + head // 2
    zone, side = seq // 2, seq % 2
    place = jnp.stack([mine, zone, side]).astype(jnp.int32)
    loss_weight = float(length * places * D // 8)
    row_shape = (quarter, D)
    window_shape = (DK + 16, 2 * DK)


    waiting = []

    def run(body, args, outs, scratch=(), vmem=6):
        micros = COST.get(getattr(body, "func", body).__name__, 1.0)
        gate = after(place, *waiting) if waiting else place
        made = call(body, gate, args, outs, scratch, vmem, micros)
        waiting[:] = [made[-1]]
        return made

    def hold(*xs):
        waiting.extend(xs)
        return xs[0] if len(xs) == 1 else xs

    def ready(x):
        return after(x, *waiting)

    def own(x):
        return lax.dynamic_slice_in_dim(x, mine * quarter, quarter, 0)

    def fold(sent, kept):
        got = flip(sent, "head", 1)
        return run(fold_kernel, [kept, got], [(row_shape, F32), (row_shape, BF16)])

    def cut(own_rows, by):
        target = lax.rem(zone + by, turns)
        return lax.dynamic_slice_in_dim(own_rows, target * pair, pair, 1)

    def quarters(own_rows, side_rows):
        return [own_rows, side_rows, flip(own_rows, "head", 1), flip(side_rows, "head", 1)]

    start_row = starts.astype(F32).reshape(1, length)
    input_float = block_input.astype(F32)
    normed = (input_float * root_scale(input_float) * first_gain).astype(BF16)
    pre_k = dot(normed, key_weight).astype(BF16)
    pre_v = dot(normed, value_weight).astype(BF16)
    pre_q = dot(normed, query_weight).astype(BF16)
    last_start, before_last = start_row[0, length - 1], start_row[0, length - 2]
    keep_one = 1.0 - last_start
    tail_keep = jnp.concatenate(
        [jnp.zeros((5,), F32), jnp.stack([keep_one * (1.0 - before_last), keep_one, jnp.ones((), F32)])]
    )
    tails = jnp.concatenate([pre_q[length - 8 :], pre_k[length - 8 :], pre_v[length - 8 :]], axis=1)
    edge = shift(tails * tail_keep[:, None].astype(BF16), "seq", 1)
    taps = jnp.concatenate([query_conv, key_conv, value_conv], axis=1)
    low_rank = dot(normed, lowrank_down).astype(BF16)
    u, v, x, logit, window = run(
        state_kernel,
        [pre_q, pre_k, pre_v, edge, taps, start_row, low_rank, lowrank_up, decay_bias.reshape(1, DK)],
        [
            ((length, channels), F32),
            ((length, DV), BF16),
            ((length, DK), F32),
            ((length, DK), F32),
            (window_shape, BF16),
        ],
        [((length + 8, channels), F32)],
    )

    def carry(window, sign, beside):
        found = None
        step, at = 1, 0
        while step < places:
            last = 2 * step >= places
            got = shift(window, "seq", sign * step)
            got, *_ = beside(at, step, got, window)
            args = [got] + ([] if last else [window]) + ([] if found is None else [found])
            outs = [((DK, DV), BF16)] if last else [(window_shape, BF16), (window_shape, BF16)]
            made = run(functools.partial(carry_kernel, found is None, last), args, outs)
            if not last:
                window, found = made
            step, at = 2 * step, at + 1
        return made[0]

    def finish(blocks):
        while len(blocks) < turns - 1:
            blocks.append(turn(blocks[-1], 1))
        return blocks

    valid_float = valid_mask.astype(F32)
    normed_own = own(normed)
    counts, normed_got, outgates = [jnp.full((8, 128), jnp.sum(valid_float), F32)], [], []

    def with_forward(at, step, got, window):
        count = after(counts[-1], window)
        beside = [count + flip(count, "seq", step)]
        if at + 1 < turns:
            beside.append(turn(after(cut(normed_own, at + 1), window), at + 1))
        if at == 0:
            beside.append(dot(after(normed, window), outgate_weight))
        got, *beside = join(got, *beside)
        counts.append(beside[0])
        normed_got.extend(beside[1:2])
        outgates.extend(beside[2:])
        return (got,)

    state_in = carry(window, 1, with_forward)
    outgate, valid_count = outgates[0], counts[-1][0:1, 0:1]
    for by in range(len(normed_got) + 1, turns):
        normed_got.append(turn(cut(normed_own, by), by))
    gain_row = outnorm_gain.reshape(1, DV)
    second_row = second_gain.reshape(1, D)
    input_own = own(block_input)
    valid_own = own(valid_float)[:, None]
    teacher_own, cotangent_own = own(teacher), own(cotangent)
    gated, mixed, scores, sent, kept = run(
        output_kernel,
        [u, v, x, start_row, state_in, outgate, gain_row, output_weight],
        [
            ((length, DV), BF16),
            ((length, DV), F32),
            ((length, length), BF16),
            ((half, D), BF16),
            ((half, D), F32),
        ],
    )

    near, far = fold(sent, kept)
    far, turned = join(far, gated)
    far, gated_1 = join(flip(far, "head", 2), turn(turned, 1))
    hidden, ffn_own = run(
        hidden_kernel, [near, far, input_own, second_row], [(row_shape, F32), (row_shape, BF16)]
    )
    ffn_side, ffn_1 = join(flip(ffn_own, "head", 2), turn(ffn_own, 1))
    ffn_in = quarters(ffn_own, ffn_side)
    activated, gate_in, up_in, ffn_cut = run(*gate_up(pair, ffn_in, gate_weight, up_weight, BF16))
    sent, kept = run(*rows_times([activated], [(0, 0, hidden_units, down_weight)]))
    near, far = fold(sent, kept)
    far, turned = join(far, ffn_1)
    far, ffn_2 = join(flip(far, "head", 2), turn(turned, 1))
    output_own, d_out, d_ffn_own, squared = run(
        functools.partial(loss_kernel, loss_weight),
        [near, far, hidden, teacher_own, cotangent_own, valid_own, valid_count],
        [(row_shape, BF16), (row_shape, F32), (row_shape, BF16), ((1, 1), F32)],
    )
    d_ffn_own, turned, turned_too = join(d_ffn_own, ffn_2, gated_1)
    d_ffn_side, ffn_3, gated_2 = join(
        flip(d_ffn_own, "head", 2), turn(turned, 1), turn(turned_too, 1)
    )
    d_ffn = quarters(d_ffn_own, d_ffn_side)
    d_gate, d_up, d_ffn_cut = run(*gate_back_rows(pair, d_ffn, down_weight, gate_in, up_in))
    sent, kept = run(
        *rows_times(
            [d_gate, d_up],
            [(0, 0, hidden_units, gate_weight), (1, 0, hidden_units, up_weight)],
        )
    )
    near, far = fold(sent, kept)
    far, turned = join(far, d_ffn_own)
    far, d_1 = join(flip(far, "head", 2), turn(turned, 1))
    d_hidden, d_branch_own, second_part = run(
        hidden_back_kernel,
        [near, far, hidden, d_out, second_row],
        [(row_shape, F32), (row_shape, BF16), ((1, D), F32)],
    )
    d_branch_own, turned, turned_too = join(d_branch_own, d_1, gated_2)
    d_branch_side, d_2, gated_3 = join(
        flip(d_branch_own, "head", 2), turn(turned, 1), turn(turned_too, 1)
    )
    d_branch = quarters(d_branch_own, d_branch_side)

    d_outgate, d_mixed, outnorm_part, direct, branch_cut = run(
        gate_back_kernel,
        [*d_branch, output_weight, mixed, outgate, gain_row, u, x, start_row],
        [
            ((length, DV), BF16),
            ((length, DV), BF16),
            ((1, DV), F32),
            (window_shape, BF16),
            ((length, pair), BF16),
        ],
        [((length, D), BF16)],
    )

    made, grads = [], []

    def far_forward(own_rows, side_rows):
        made.append(run(*gate_up(pair, quarters(own_rows, side_rows), gate_weight, up_weight, BF16)))

    def far_back(own_rows, side_rows):
        part = made[len(grads)]
        pieces = quarters(own_rows, side_rows)
        grads.append(run(*gate_back_rows(pair, pieces, down_weight, part[1], part[2])))

    ffn_turns, d_turns = finish([ffn_1, ffn_2, ffn_3]), [d_1, d_2]
    gated_turns = finish([gated_1, gated_2, gated_3])
    ffn_sides, d_sides, outgate_turns, branch_got, sums = [], [], [], [], {}

    def weigh(name, lefts, rights):
        sums[name] = run(*weight_args("cuts", share, lefts, rights), vmem=8)

    def with_back(at, step, got, window):
        if at == 0:
            ffn_sides.extend(flip(after(r, window), "head", 2) for r in (ffn_1, ffn_2))
            d_turns.append(turn(after(d_2, window), 1))
            hold(*ffn_sides, d_turns[2])
        elif at == 1:
            ffn_sides.append(flip(after(ffn_3, window), "head", 2))
            d_sides.append(flip(after(d_1, window), "head", 2))
            outgate_turns.append(turn(after(d_outgate, window), 1))
            far_forward(ffn_1, ffn_sides[0])
            far_forward(ffn_2, ffn_sides[1])
            hold(ffn_sides[2], *d_sides, *outgate_turns)
        elif at == 2:
            d_sides.extend(flip(after(r, window), "head", 2) for r in (d_2, d_turns[2]))
            outgate_turns.append(turn(after(outgate_turns[-1], window), 1))
            branch_got.extend(
                turn(after(cut(d_branch_own, by), window), by) for by in range(1, turns)
            )
            far_forward(ffn_3, ffn_sides[2])
            far_back(d_1, d_sides[0])
            hold(*d_sides[1:], outgate_turns[-1], *branch_got)
        return (got,)

    later = carry(direct, -1, with_back)
    d_pre, last_rows, pack, d_low, back_rows = run(
        mixer_back_kernel,
        [
            d_mixed, state_in, later, u, v, x, scores, pre_q, pre_k, pre_v, edge, taps,
            logit, start_row, low_rank, lowrank_up,
        ],
        [
            ((length, channels), BF16),
            ((8, channels), F32),
            ((8, D), F32),
            ((RANK, length), F32),
            ((8, channels), F32),
        ],
        [
            ((length + 8, channels), F32),
            ((length + 8, channels), F32),
            ((16, DK), F32),
            ((length, DK), F32),
        ],
        vmem=7,
    )

    from_next = shift(back_rows, "seq", -1)
    outgate_turns.append(turn(after(outgate_turns[-1], back_rows), 1))
    far_back(d_2, d_sides[1])
    far_back(d_turns[2], d_sides[2])
    finish(d_turns)
    for extra in range(3, turns - 1):
        far_forward(ffn_turns[extra], flip(ffn_turns[extra], "head", 2))
        far_back(d_turns[extra], flip(d_turns[extra], "head", 2))
    hold(outgate_turns[-1])
    fixed = (last_rows + from_next * tail_keep[:, None]).astype(BF16)
    d_pre = lax.dynamic_update_slice(d_pre, fixed, ((mine ^ 3) * quarter + quarter - 8, 0))

    pre_1 = turn(d_pre, 1)

    def across(sums, *gates):
        return sums[0], flip(after(sums[0], *gates), "seq", 1), sums[1]

    sent, kept = run(
        *rows_times(
            [d_outgate, d_pre],
            [
                (0, 0, DV, outgate_weight),
                (1, 0, DK, query_weight),
                (1, DK, DK, key_weight),
                (1, 2 * DK, DV, value_weight),
            ],
        )
    )
    d_low = after(d_low, *waiting)
    near, far = fold(sent, kept)
    far = flip(far, "head", 2)
    d_lowrank = total(d_low, [("head", 1), ("head", 2)]).astype(BF16)
    low_own = lax.dynamic_slice_in_dim(d_lowrank, mine * quarter, quarter, 1)
    cuts = [ffn_cut, *(f[3] for f in made)]
    weigh("gate", cuts, [d_gate, *(g[0] for g in grads)])
    moved_gate = across(sums["gate"])
    weigh("up", cuts, [d_up, *(g[1] for g in grads)])
    moved_up = across(sums["up"])
    hold(pre_1)
    grad_own, first_part = run(
        input_back_kernel,
        [near, far, input_own, d_hidden, first_gain.reshape(1, D), low_own, lowrank_down.T],
        [(row_shape, BF16), ((1, D), F32)],
    )
    pre_2 = turn(ready(pre_1), 1)
    weigh("down", [d_ffn_cut, *(g[2] for g in grads)], [activated, *(f[0] for f in made)])
    moved_down = across(sums["down"])
    branch_near = after(jnp.concatenate(branch_got, axis=0), grad_own)
    branch_far = quarters(branch_near, flip(branch_near, "head", 2))
    normed_near = after(jnp.concatenate(normed_got, axis=0), grad_own)
    normed_far = quarters(normed_near, flip(normed_near, "head", 2))
    grad_side = flip(after(grad_own, branch_near), "head", 2)
    sum_output = run(*weight_args("stacked", share, [branch_cut, *branch_far], [gated, *gated_turns]))
    sum_outgate = run(
        *weight_args("natural", share, [normed, *normed_far], [d_outgate, *finish(outgate_turns)])
    )
    (apart,) = run(low_kernel, [d_lowrank, normed, pack], [((RANK + 8, D), F32)])
    odd = jnp.concatenate(
        [outnorm_part, jnp.broadcast_to(squared, (1, DV)), jnp.zeros((1, D - 2 * DV), F32)], axis=1
    )
    shared = jnp.concatenate([first_part, second_part, odd], axis=0)
    upper = [("seq", bit) for bit in (1 << p for p in range(1, 16)) if bit < places]
    hold(pre_2, grad_side, moved_gate[1])
    (grad_input,) = run(natural_kernel, quarters(grad_own, grad_side), [((length, D), F32)])
    pre_3 = turn(ready(pre_2), 1)
    moved_output, moved_outgate = across(sum_output, pre_2), across(sum_outgate, pre_2)
    output_later = after(output_own, pre_2)
    output_side = flip(output_later, "head", 2)
    shared = total(after(shared, pre_2), [("head", 1), ("head", 2)])
    apart = total(after(apart, pre_2), upper, BF16)
    hold(moved_up[1])
    (block_output,) = run(natural_kernel, quarters(output_later, output_side), [((length, D), F32)])
    sum_pre = run(
        *weight_args(
            "natural", share, [normed, *normed_far], [d_pre, *finish([pre_1, pre_2, pre_3])]
        )
    )
    moved_pre = flip(sum_pre[0], "seq", 1)
    shared = total(after(shared, sum_pre[0]), [*upper, ("seq", 1)])
    apart = total(after(apart, sum_pre[0]), [("seq", 1)], BF16)
    grad_gate, grad_up, grad_down, grad_output, grad_outgate = (
        kept + after(got, sum_pre[0]).astype(F32)
        for _, got, kept in (moved_gate, moved_up, moved_down, moved_output, moved_outgate)
    )
    grad_query, grad_key, grad_value = run(
        settle_kernel, [sum_pre[1], moved_pre],
        [((share, DK), F32), ((share, DK), F32), ((share, DV), F32)],
    )
    taps_query, taps_key, taps_value, grad_lowrank_up, bias_row, down_row = run(
        functools.partial(unpack_kernel, share),
        [apart],
        [
            ((TAPS, DK), F32),
            ((TAPS, DK), F32),
            ((TAPS, DV), F32),
            ((RANK, DK), F32),
            ((1, DK), F32),
            ((RANK, share), F32),
        ],
    )
    distill = shared[2, DV] / (valid_count[0, 0] * D)
    return (
        block_output,
        distill,
        grad_input,
        shared[0],
        grad_query,
        grad_key,
        grad_value,
        taps_query,
        taps_key,
        taps_value,
        down_row.T,
        grad_lowrank_up,
        bias_row.reshape(DK),
        grad_outgate,
        shared[2, :DV],
        grad_output,
        shared[1],
        grad_gate,
        grad_up,
        grad_down,
    )


def solution(mesh):
    rows, cols, whole = P("seq", None), P(None, "head"), P()
    in_specs = (
        rows, whole, cols, cols, cols, cols, cols, cols, whole, cols, P("head"), cols, whole, cols,
        whole, cols, cols, cols, P("seq"), P("seq"), rows, rows,
    )
    tiles = P("seq", "head")
    out_specs = (
        rows, whole, rows, whole, tiles, tiles, tiles, cols, cols, cols, rows, cols, P("head"), tiles,
        whole, tiles, whole, tiles, tiles, tiles,
    )
    return jax.shard_map(
        on_device, mesh=mesh, in_specs=in_specs, out_specs=out_specs, check_vma=False
    )
```

```python
import functools

import functools

import jax
import jax.numpy as jnp
from jax import lax
from jax.experimental import pallas as pl
from jax.experimental.pallas import tpu as pltpu
from jax.sharding import PartitionSpec as P

D = 2048
DK = 256
DV = 512
RANK = 16
TAPS = 4
BLOCK = 64
EPSILON = 1e-05
HIGHEST = lax.Precision.HIGHEST
F32 = jnp.float32
BF16 = jnp.bfloat16
MIB = 1024 * 1024


def contract_rows(left, right):
    return lax.dot_general(left, right, (((0,), (0,)), ((), ())), preferred_element_type=F32)


def contract_cols(left, right):
    return lax.dot_general(left, right, (((1,), (1,)), ((), ())), preferred_element_type=F32)


def dot(left, right, precision=None):
    return lax.dot_general(
        left, right, (((1,), (0,)), ((), ())), precision=precision, preferred_element_type=F32
    )


def root_scale(v):
    return lax.rsqrt(jnp.mean(v * v, axis=-1, keepdims=True) + EPSILON)


def norm_backward(v, scale, gain, upstream):
    scaled_up = upstream * gain
    return scale * scaled_up - v * scale * scale * scale * jnp.mean(
        scaled_up * v, axis=-1, keepdims=True
    )


def flip(x, axis, bit):
    n = lax.axis_size(axis)
    return lax.ppermute(x, axis, [(i, i ^ bit) for i in range(n)])


def shift(x, axis, by):
    n = lax.axis_size(axis)
    return lax.ppermute(x, axis, [(i, i + by) for i in range(n) if 0 <= i + by < n])


def turn(x, by):
    n = lax.axis_size("seq")
    return lax.ppermute(x, "seq", [(i, (i + 2 * by) % n) for i in range(n)])


def after(x, *others):
    return lax.optimization_barrier((x, *others))[0]


def join(*xs):
    return lax.optimization_barrier(xs)


def total(x, steps, kind=F32):
    for axis, bit in steps:
        if kind != F32:
            x = lax.reduce_precision(x, 8, 7)
        x = x + flip(x.astype(kind), axis, bit).astype(F32)
    return x


def grids(n):
    return (
        lax.broadcasted_iota(jnp.int32, (n, n), 0),
        lax.broadcasted_iota(jnp.int32, (n, n), 1),
    )


def column(row, rows, cols, back):
    return jnp.sum(jnp.where(cols == rows - back, row, 0.0), axis=1, keepdims=True)


def tap_masks(start_row, rows, cols):
    here, one, two = (column(start_row, rows, cols, back) for back in range(3))
    first = 1.0 - here
    second = first * (1.0 - one)
    return here, (first, second, second * (1.0 - two))


def segments(start_row, start_col, rows, cols):
    seg_col = jnp.sum(jnp.where(cols <= rows, start_row, 0.0), axis=1, keepdims=True)
    seg_row = jnp.sum(jnp.where(rows <= cols, start_col, 0.0), axis=0, keepdims=True)
    return seg_col, seg_row, jnp.sum(start_row)


def block_middles(x):
    n = x.shape[0] // BLOCK
    mids = []
    for b in range(n):
        last = x[(b + 1) * BLOCK - 1 : (b + 1) * BLOCK]
        before = x[b * BLOCK - 1 : b * BLOCK] if b else jnp.zeros_like(last)
        mids.append(0.5 * (before + last))
    return mids


def spread(mids):
    return jnp.concatenate(
        [jnp.broadcast_to(mid, (BLOCK, mid.shape[1])) for mid in mids], axis=0
    )


def state_kernel(
    place, pre_q, pre_k, pre_v, edge, taps, start_row, low_rank, lowrank_up, bias,
    u_out, v_out, x_out, logit_out, state_out, ext,
):
    n = pre_q.shape[0]
    rows, cols = grids(n)
    sr = start_row[...]
    start_col, masks = tap_masks(sr, rows, cols)
    seg_col, _, seg_last = segments(sr, start_col, rows, cols)
    ext[0:8, :] = edge[...].astype(F32)
    ext[8:, 0:DK] = pre_q[...].astype(F32)
    ext[8:, DK : 2 * DK] = pre_k[...].astype(F32)
    ext[8:, 2 * DK :] = pre_v[...].astype(F32)
    for part in range(4):
        lanes = slice(part * DK, (part + 1) * DK)
        u = ext[8 : 8 + n, lanes] * taps[3:4, lanes]
        for back in range(1, TAPS):
            u = u + ext[8 - back : 8 - back + n, lanes] * taps[3 - back : 4 - back, lanes] * masks[
                back - 1
            ]
        u_out[:, lanes] = u
        if part >= 2:
            v_out[:, (part - 2) * DK : (part - 1) * DK] = (u * jax.nn.sigmoid(u)).astype(BF16)
    logit = dot(low_rank[...], lowrank_up[...]) + bias[...]
    logit_out[...] = logit
    decays = (jnp.minimum(logit, 0.0) - jnp.log1p(jnp.exp(-jnp.abs(logit)))) * (1.0 / 16.0)
    x = dot((cols <= rows).astype(F32), decays, HIGHEST)
    x_out[...] = x
    u = u_out[:, DK : 2 * DK]
    keys = u * jax.nn.sigmoid(u)
    tail = (seg_col == seg_last).astype(F32)
    final = x[n - 1 : n]
    closing = (keys * jnp.exp(final - x) * tail).astype(BF16)
    put_decay(
        state_out,
        contract_rows(closing, v_out[...]).astype(BF16),
        jnp.exp(final) * (seg_last == 0.0).astype(F32),
    )


def local_scores(q, k, x):
    n = x.shape[0] // BLOCK
    mids = block_middles(x)
    mid = spread(mids)
    grow, shrink = jnp.exp(x - mid), jnp.exp(mid - x)
    rising, falling = q * grow, (k * shrink).astype(BF16)
    lifted, scales = [], []
    for j in range(n):
        pieces = [jnp.exp(mids[i] - mids[j]) for i in range(j, n)]
        scale = spread(pieces)
        scales.append(scale)
        lifted.append((rising[j * BLOCK :] * scale).astype(BF16))
    return grow, shrink, lifted, scales, falling


def output_kernel(
    place, u_qk, v, x_in, start_row, state_in, outgate, gain, weight,
    gated_out, mixed_out, scores_out, sent_out, kept_out,
):
    n = x_in.shape[0]
    blocks = n // BLOCK
    rows, cols = grids(n)
    sr = start_row[...]
    start_col = column(sr, rows, cols, 0)
    seg_col, seg_row, _ = segments(sr, start_col, rows, cols)
    allowed = (cols <= rows) & (seg_col == seg_row)
    alive = (seg_col == 0.0).astype(F32)
    x = x_in[...]
    uq = u_qk[:, 0:DK]
    uk = u_qk[:, DK : 2 * DK]
    q = uq * jax.nn.sigmoid(uq) * DK**-0.5
    k = uk * jax.nn.sigmoid(uk)
    _, _, lifted, _, falling = local_scores(q, k, x)
    scores_out[...] = jnp.zeros_like(scores_out)
    for j in range(blocks):
        lo, hi = j * BLOCK, (j + 1) * BLOCK
        s = contract_cols(lifted[j], falling[lo:hi])
        scores_out[lo:, lo:hi] = jnp.where(allowed[lo:, lo:hi], s, 0.0).astype(BF16)
    carried = (q * jnp.exp(x) * alive).astype(BF16)
    out = dot(scores_out[...], v[...]) + dot(carried, state_in[...])
    mixed_out[...] = out
    og = outgate[...]
    gated = (out * root_scale(out) * gain[...] * (og * jax.nn.sigmoid(og))).astype(BF16)
    m = place[0]
    for b in range(blocks):
        at = pl.multiple_of((m ^ b) * BLOCK, BLOCK)
        gated_out[pl.ds(at, BLOCK), :] = gated[b * BLOCK : (b + 1) * BLOCK]
    half = n // 2
    for part in range(4):
        lanes = slice(part * DV, (part + 1) * DV)
        branch = contract_cols(gated_out[...], weight[lanes, :])
        kept_out[:, lanes] = branch[0:half]
        sent_out[:, lanes] = branch[half:].astype(BF16)


def gate_back_kernel(
    place, branch_0, branch_1, branch_2, branch_3, weight, mixed, outgate, gain, u_in, x_in,
    start_row, d_outgate_out, d_mixed_out, gain_out, direct_out, order,
):
    n = x_in.shape[0]
    blocks = n // BLOCK
    m = place[0]
    for p, piece in enumerate((branch_0, branch_1, branch_2, branch_3)):
        at = pl.multiple_of((m ^ p) * BLOCK, BLOCK)
        order[pl.ds(at, BLOCK), :] = piece[...]
    up = dot(order[...], weight[...])
    og = outgate[...]
    sig = jax.nn.sigmoid(og)
    out = mixed[...]
    scale = root_scale(out)
    g = gain[...]
    d_outgate = (up * (out * scale * g) * sig * (1.0 + og * (1.0 - sig))).astype(BF16)
    for b in range(blocks):
        at = pl.multiple_of((m ^ b) * BLOCK, BLOCK)
        d_outgate_out[pl.ds(at, BLOCK), :] = d_outgate[b * BLOCK : (b + 1) * BLOCK]
    d_norm = up * (og * sig)
    gain_out[...] = jnp.sum(d_norm * out * scale, axis=0, keepdims=True)
    d_mixed = norm_backward(out, scale, g, d_norm).astype(BF16)
    d_mixed_out[...] = d_mixed
    rows, cols = grids(n)
    sr = start_row[...]
    seg_col = jnp.sum(jnp.where(cols <= rows, sr, 0.0), axis=1, keepdims=True)
    alive = (seg_col == 0.0).astype(F32)
    uq = u_in[:, 0:DK]
    x = x_in[...]
    carried = (uq * jax.nn.sigmoid(uq) * DK**-0.5 * jnp.exp(x) * alive).astype(BF16)
    put_decay(
        direct_out,
        contract_rows(carried, d_mixed).astype(BF16),
        jnp.exp(x[n - 1 : n]) * (jnp.sum(sr) == 0.0).astype(F32),
    )


def mixer_back_kernel(
    place, d_mixed, state_in, later, u_in, v, x_in, scores, pre_q, pre_k, pre_v, edge, taps,
    logit, start_row, low_rank, lowrank_up,
    d_pre_out, last_rows_out, pack_out, d_low_out, back_rows_out,
    ext, du_ext, small, dx_buf,
):
    n = x_in.shape[0]
    blocks = n // BLOCK
    m = place[0]
    rows, cols = grids(n)
    sr = start_row[...]
    start_col, masks = tap_masks(sr, rows, cols)
    seg_col, seg_row, seg_last = segments(sr, start_col, rows, cols)
    allowed = (cols <= rows) & (seg_col == seg_row)
    alive = (seg_col == 0.0).astype(F32)
    tail = (seg_col == seg_last).astype(F32)
    x = x_in[...]
    uq = u_in[:, 0:DK]
    uk = u_in[:, DK : 2 * DK]
    sq, sk = jax.nn.sigmoid(uq), jax.nn.sigmoid(uk)
    q = uq * sq * DK**-0.5
    k = uk * sk
    grow, shrink, lifted, scales, falling = local_scores(q, k, x)
    dm = d_mixed[...]
    later_b = later[...]
    later_f = later_b.astype(F32)
    state_f = state_in[...].astype(F32)
    d_scores = jnp.where(allowed, contract_cols(dm, v[...]), 0.0).astype(BF16)
    final = x[n - 1 : n]
    leaving = jnp.exp(final - x) * tail
    closing = (k * leaving).astype(BF16)
    d_closing = contract_cols(v[...], later_b)
    entering = jnp.exp(x) * alive
    d_carried = contract_cols(dm, state_in[...])
    dq = d_carried * entering
    dk = d_closing * leaving
    closed = d_closing * closing.astype(F32)
    dx_buf[...] = d_carried * (q * entering) - closed
    through = jnp.sum(later_f * state_f, axis=1, keepdims=True)
    through_row = jnp.sum(jnp.where(rows == cols, through, 0.0), axis=0, keepdims=True)
    at_last = jnp.sum(closed, axis=0, keepdims=True) + through_row * jnp.exp(final) * (
        seg_last == 0.0
    ).astype(F32)
    dx_buf[n - 1 : n, :] = dx_buf[n - 1 : n, :] + at_last
    dq_parts = [dq[b * BLOCK : (b + 1) * BLOCK] for b in range(blocks)]
    dk_parts = []
    for j in range(blocks):
        lo, hi = j * BLOCK, (j + 1) * BLOCK
        ds = d_scores[lo:, lo:hi]
        d_lift = dot(ds, falling[lo:hi])
        d_fall = contract_rows(ds, lifted[j])
        dx_buf[lo:, :] = dx_buf[lo:, :] + d_lift * lifted[j].astype(F32)
        dx_buf[lo:hi, :] = dx_buf[lo:hi, :] - d_fall * falling[lo:hi].astype(F32)
        d_rise = d_lift * scales[j] * grow[lo:]
        for b in range(j, blocks):
            dq_parts[b] = dq_parts[b] + d_rise[(b - j) * BLOCK : (b - j + 1) * BLOCK]
        dk_parts.append(dk[lo:hi] + d_fall * shrink[lo:hi])
    dq = jnp.concatenate(dq_parts, axis=0)
    dk = jnp.concatenate(dk_parts, axis=0)
    d_decays = dot((cols >= rows).astype(F32), dx_buf[...], HIGHEST)
    d_logit = (d_decays * jax.nn.sigmoid(-logit[...]) * (1.0 / 16.0)).astype(BF16)
    pack_out[...] = jnp.zeros_like(pack_out)
    pack_out[4:5, 0:DK] = jnp.sum(d_logit.astype(F32), axis=0, keepdims=True)
    d_up = contract_rows(low_rank[...], d_logit)
    per = pack_out.shape[1] // DK
    for row in range(RANK):
        at = (row % per) * DK
        pack_out[2 + row // per : 3 + row // per, at : at + DK] = d_up[row : row + 1]
    d_low_out[...] = contract_cols(lowrank_up[...], d_logit)

    ext[0:8, :] = edge[...].astype(F32)
    ext[8:, 0:DK] = pre_q[...].astype(F32)
    ext[8:, DK : 2 * DK] = pre_k[...].astype(F32)
    ext[8:, 2 * DK :] = pre_v[...].astype(F32)
    du_ext[n:, :] = jnp.zeros((8, du_ext.shape[1]), F32)
    du_ext[0:n, 0:DK] = dq * (DK**-0.5) * (sq * (1.0 + uq * (1.0 - sq)))
    du_ext[0:n, DK : 2 * DK] = dk * (sk * (1.0 + uk * (1.0 - sk)))
    dv = contract_rows(scores[...], dm) + dot(closing, later_b)
    for half in range(2):
        uv = u_in[:, (2 + half) * DK : (3 + half) * DK]
        sv = jax.nn.sigmoid(uv)
        du_ext[0:n, (2 + half) * DK : (3 + half) * DK] = dv[:, half * DK : (half + 1) * DK] * (
            sv * (1.0 + uv * (1.0 - sv))
        )
    ahead = []
    for back in range(1, TAPS):
        mask_row = jnp.sum(jnp.where(rows == cols, masks[back - 1], 0.0), axis=0, keepdims=True)
        ahead.append(column(mask_row, rows, cols, -back))
    for part in range(4):
        lanes = slice(part * DK, (part + 1) * DK)
        du = du_ext[0:n, lanes]
        d_pre = du * taps[3:4, lanes]
        back_rows = jnp.zeros((8, DK), F32)
        wide = du_ext.shape[1]
        pack_out[1:2, wide + part * DK : wide + (part + 1) * DK] = jnp.sum(
            du * ext[8 : 8 + n, lanes], axis=0, keepdims=True
        )
        for back in range(1, TAPS):
            weight = taps[3 - back : 4 - back, lanes]
            d_pre = d_pre + du_ext[back : back + n, lanes] * weight * ahead[back - 1]
            masked = du * masks[back - 1]
            row, at = (3 - back) // 2, (3 - back) % 2 * wide + part * DK
            pack_out[row : row + 1, at : at + DK] = jnp.sum(
                masked * ext[8 - back : 8 - back + n, lanes], axis=0, keepdims=True
            )
            small[0:8, :] = jnp.zeros((8, DK), F32)
            small[8:16, :] = masked[0:8]
            back_rows = back_rows + small[back : back + 8, :] * weight
        back_rows_out[:, lanes] = back_rows
        last_rows_out[:, lanes] = d_pre[n - 8 :]
        rounded = d_pre.astype(BF16)
        for b in range(blocks):
            at = pl.multiple_of((m ^ b) * BLOCK, BLOCK)
            d_pre_out[pl.ds(at, BLOCK), lanes] = rounded[b * BLOCK : (b + 1) * BLOCK]


def whole_spec():
    return pl.BlockSpec(memory_space=pltpu.VMEM)


def call(body, place, args, outs, scratch=(), vmem=6, micros=1.0):
    return pl.pallas_call(
        body,
        out_shape=[jax.ShapeDtypeStruct(shape, kind) for shape, kind in outs],
        in_specs=[pl.BlockSpec(memory_space=pltpu.SMEM)] + [whole_spec() for _ in args],
        out_specs=[whole_spec() for _ in outs],
        scratch_shapes=[pltpu.VMEM(shape, kind) for shape, kind in scratch],
        compiler_params=pltpu.CompilerParams(vmem_limit_bytes=vmem * MIB),
        cost_estimate=pl.CostEstimate(
            flops=int(micros * 1e9), bytes_accessed=int(micros * 3e6), transcendentals=0
        ),
    )(place, *args)


def spans(width, tile):
    return [slice(at, min(at + tile, width)) for at in range(0, width, tile)]


def fold_kernel(place, kept, got, near_out, far_out):
    quarter = near_out.shape[0]
    near_out[...] = kept[0:quarter] + got[0:quarter].astype(F32)
    far_out[...] = (kept[quarter:] + got[quarter:].astype(F32)).astype(BF16)


def own_rows(place, ref, quarter):
    return ref[pl.ds(pl.multiple_of(place[0] * quarter, quarter), quarter), :]


def hidden_kernel(place, kept, got, rows, gain, hidden_out, ffn_out):
    hidden = own_rows(place, rows, kept.shape[0]).astype(F32) + (kept[...] + got[...].astype(F32))
    hidden_out[...] = hidden
    ffn_out[...] = (hidden * root_scale(hidden) * gain[...]).astype(BF16)


def loss_kernel(
    weight, place, kept, got, hidden, teacher, cotangent, valid, count,
    output_out, d_out_out, d_ffn_out, squared_out,
):
    quarter = kept.shape[0]
    output = hidden[...] + (kept[...] + got[...].astype(F32))
    output_out[...] = output.astype(BF16)
    mismatch = output - own_rows(place, teacher, quarter).astype(F32)
    length = valid.shape[1]
    rows = lax.broadcasted_iota(jnp.int32, (quarter, length), 0) + place[0] * quarter
    cols = lax.broadcasted_iota(jnp.int32, (quarter, length), 1)
    keep = jnp.sum(jnp.where(rows == cols, valid[...], 0.0), axis=1, keepdims=True)
    squares = jnp.sum(keep * mismatch * mismatch, axis=0, keepdims=True)
    squared_out[...] = jnp.sum(squares, axis=1, keepdims=True)
    scaled = keep * (2.0 * weight) * mismatch / (count[0:1, 0:1] * D)
    d_out = own_rows(place, cotangent, quarter).astype(F32) + scaled
    d_out_out[...] = d_out
    d_ffn_out[...] = d_out.astype(BF16)


def hidden_back_kernel(
    turns, place, kept, got, hidden, d_out, gain, normed, d_hidden_out, d_branch_out, gain_out, *cuts
):
    d_norm = kept[...] + got[...].astype(F32)
    h = hidden[...]
    scale = root_scale(h)
    gain_out[...] = jnp.sum(d_norm * h * scale, axis=0, keepdims=True)
    d_hidden = d_out[...] + norm_backward(h, scale, gain[...], d_norm)
    d_hidden_out[...] = d_hidden
    d_branch_out[...] = d_hidden.astype(BF16)
    quarter = kept.shape[0]
    rows = pl.ds(pl.multiple_of(place[0] * quarter, quarter), quarter)
    for by, cut in enumerate(cuts, 1):
        pair = cut.shape[1] // 2
        target = place[1] + by
        target = jnp.where(target >= turns, target - turns, target)
        lanes = pl.ds(pl.multiple_of(target * pair, pair), pair)
        cut[:, 0:pair] = normed[rows, lanes]
        cut[:, pair:] = d_branch_out[:, lanes]


def input_back_kernel(
    place, kept, got, rows, d_hidden, gain, d_low, d_low_got, down_turned,
    grad_out, gain_out, d_low_out,
):
    quarter, length = kept.shape[0], d_low.shape[1]
    d_lowrank = (d_low[...] + d_low_got[...]).astype(BF16)
    d_low_out[...] = d_lowrank
    here = lax.broadcasted_iota(jnp.int32, (quarter, length), 0) + place[0] * quarter
    tokens = lax.broadcasted_iota(jnp.int32, (quarter, length), 1)
    own_low = contract_cols((here == tokens).astype(BF16), d_lowrank).astype(BF16)
    d_norm = (kept[...] + got[...].astype(F32)) + dot(own_low, down_turned[...])
    v = own_rows(place, rows, quarter).astype(F32)
    scale = root_scale(v)
    gain_out[...] = jnp.sum(d_norm * v * scale, axis=0, keepdims=True)
    grad_out[...] = (d_hidden[...] + norm_backward(v, scale, gain[...], d_norm)).astype(BF16)


def carry_kernel(first, last, place, got, *refs):
    refs = list(refs)
    window = None if last else refs.pop(0)
    found = None if first else refs.pop(0)
    n = DK
    rows, cols = grids(n)

    def as_column(row):
        return jnp.sum(jnp.where(rows == cols, row, 0.0), axis=1, keepdims=True)

    def decay_of(ref):
        both = ref[n : n + 1, :].astype(F32)
        return both[:, 0:n] + both[:, n : 2 * n]

    arrived = got[0:n, :].astype(F32)
    if first:
        merged = arrived
        found_decay = decay_of(got)
    else:
        own = decay_of(found)
        merged = as_column(own) * arrived + found[0:n, :].astype(F32)
        found_decay = own * decay_of(got)
    if last:
        refs.pop(0)[...] = merged.astype(BF16)
        return
    window_decay = decay_of(window)
    state = as_column(window_decay) * arrived + window[0:n, :].astype(F32)
    put_decay(refs.pop(0), state.astype(BF16), window_decay * decay_of(got))
    put_decay(refs.pop(0), merged.astype(BF16), found_decay)


def put_decay(ref, state, decay):
    n = DK
    ref[0:n, :] = state
    high = decay.astype(BF16)
    low = (decay - high.astype(F32)).astype(BF16)
    row = jnp.concatenate([high, low], axis=1)
    ref[n:, :] = jnp.broadcast_to(row, (ref.shape[0] - n, 2 * n))


def rows_kernel(count, widths, place, *refs):
    lefts, rights = refs[:count], refs[count : count + len(widths)]
    sent, kept = refs[count + len(widths) :]
    half = sent.shape[0]
    for lanes in spans(kept.shape[1], 1024):
        acc = None
        for (left, at, width), right in zip(widths, rights):
            term = contract_cols(lefts[left][:, at : at + width], right[lanes, :])
            acc = term if acc is None else acc + term
        kept[:, lanes] = acc[0:half]
        sent[:, lanes] = acc[half:].astype(BF16)


def rows_times(lefts, pairs):
    half = lefts[0].shape[0] // 2
    widths = [pair[:3] for pair in pairs]
    return (
        functools.partial(rows_kernel, len(lefts), widths),
        [*lefts, *(pair[3] for pair in pairs)],
        [((half, D), BF16), ((half, D), F32)],
    )


def stack(pieces, buf):
    at = 0
    for piece in pieces:
        buf[at : at + piece.shape[0], :] = piece[...]
        at += piece.shape[0]


def pair_lanes(place, cut_out):
    pair = cut_out.shape[1]
    return pl.ds(pl.multiple_of(place[1] * pair, pair), pair)


def stacked(pieces, rest):
    if len(pieces) == 1:
        return pieces[0], rest
    stack(pieces, rest[-1])
    return rest[-1], rest[:-1]


def gate_parts(buf, gate_w, up_w, act_out, gate_out, up_out):
    for rows in spans(buf.shape[0], 512):
        for lanes in spans(gate_w.shape[1], 256):
            gate, up = dot(buf[rows, :], gate_w[:, lanes]), dot(buf[rows, :], up_w[:, lanes])
            sig = jax.nn.sigmoid(gate)
            swish = gate * sig
            act_out[rows, lanes] = (swish * up).astype(BF16)
            gate_out[rows, lanes] = (up * sig * (1.0 + gate * (1.0 - sig))).astype(BF16)
            up_out[rows, lanes] = swish.astype(BF16)


def gate_back_parts(buf, down_w, gate_in, up_in, d_gate_out, d_up_out):
    for rows in spans(buf.shape[0], 512):
        for lanes in spans(down_w.shape[1], 256):
            d_act = dot(buf[rows, :], down_w[:, lanes])
            d_gate_out[rows, lanes] = (d_act * gate_in[rows, lanes].astype(F32)).astype(BF16)
            d_up_out[rows, lanes] = (d_act * up_in[rows, lanes].astype(F32)).astype(BF16)


def gate_kernel(count, place, *refs):
    buf, rest = stacked(refs[:count], refs[count:])
    for cut_out in rest[5:]:
        cut_out[...] = buf[:, pair_lanes(place, cut_out)]
    gate_parts(buf, *rest[:5])


def gate_up(pieces, gate_weight, up_weight, pair=0):
    length = sum(p.shape[0] for p in pieces)
    width = gate_weight.shape[1]
    return (
        functools.partial(gate_kernel, len(pieces)),
        [*pieces, gate_weight, up_weight],
        [((length, width), BF16)] * 3 + [((length, pair), BF16)] * (pair > 0),
        [((length, D), BF16)] * (len(pieces) > 1),
    )


def gate_back_kernel_rows(count, place, *refs):
    buf, rest = stacked(refs[:count], refs[count:])
    for cut_out in rest[5:]:
        cut_out[...] = buf[:, pair_lanes(place, cut_out)]
    gate_back_parts(buf, *rest[:5])


def gate_back_rows(pieces, down_weight, gate_in, up_in, pair=0):
    length, width = gate_in.shape
    return (
        functools.partial(gate_back_kernel_rows, len(pieces)),
        [*pieces, down_weight, gate_in, up_in],
        [((length, width), BF16)] * 2 + [((length, pair), BF16)] * (pair > 0),
        [((length, D), BF16)] * (len(pieces) > 1),
    )


def zone_rows(turns, place, refs, buf):
    owns, sides = refs[:turns], []
    taken = turns
    quarter = buf.shape[0] // (2 * turns)
    while len(sides) < turns:
        ref = refs[taken]
        sides += [(ref, at) for at in range(0, ref.shape[0], quarter)]
        taken += 1
    zone = place[1]
    for by in range(turns):
        source = jnp.where(zone < by, zone - by + turns, zone - by)
        at = pl.multiple_of(2 * source * quarter, quarter)
        buf[pl.ds(at, quarter), :] = owns[by][:, 0:D]
        ref, row = sides[by]
        buf[pl.ds(at + quarter, quarter), :] = ref[row : row + quarter, :]
    return refs[taken:]


def far_gate_kernel(turns, place, *refs):
    buf = refs[-1]
    gate_w, up_w, *outs = zone_rows(turns, place, refs[:-1], buf)
    outs[3][...] = buf[:, pair_lanes(place, outs[3])]
    gate_parts(buf, gate_w, up_w, *outs[:3])


def far_gate_up(owns, sides, gate_weight, up_weight, pair):
    length, width = 2 * len(owns) * owns[0].shape[0], gate_weight.shape[1]
    return (
        functools.partial(far_gate_kernel, len(owns)),
        [*owns, *sides, gate_weight, up_weight],
        [((length, width), BF16)] * 3 + [((length, pair), BF16), ((length, D), BF16)],
    )


def far_back_kernel(turns, place, *refs):
    buf = refs[-1]
    down_w, gate_in, up_in, d_gate_out, d_up_out, cut_out = zone_rows(turns, place, refs[:-1], buf)
    cut_out[...] = buf[:, pair_lanes(place, cut_out)]
    gate_back_parts(buf, down_w, gate_in, up_in, d_gate_out, d_up_out)


def far_back_rows(owns, sides, down_weight, gate_in, up_in, pair):
    length, width = gate_in.shape
    return (
        functools.partial(far_back_kernel, len(owns)),
        [*owns, *sides, down_weight, gate_in, up_in],
        [((length, width), BF16)] * 2 + [((length, pair), BF16), ((length, D), BF16)],
    )


def pair_sums(blocks, side, sent, kept, res, at=0):
    share = kept.shape[0]
    width_all = kept.shape[1] // (2 if at or len(blocks[0]) == 4 else 1)
    for cols in spans(width_all, 256):
        acc = None
        for left, right, first, *_ in blocks:
            term = contract_rows(left[...], right[:, first + cols.start : first + cols.stop])
            acc = term if acc is None else acc + term
        width = cols.stop - cols.start
        out = slice(at + cols.start, at + cols.stop)
        res[:, 0:width] = acc
        sent[:, out] = res[
            pl.ds(pl.multiple_of((1 - side) * share, share), share), 0:width
        ].astype(BF16)
        kept[:, out] = res[pl.ds(pl.multiple_of(side * share, share), share), 0:width]


def far_weight_kernel(place, *refs):
    sent, kept, res = refs[-3:]
    count = (len(refs) - 3) // 2
    blocks = [(left, right, 0) for left, right in zip(refs[:count], refs[count:-3])]
    pair_sums(blocks, place[2], sent, kept, res)


def far_weight(share, lefts, rights):
    width = rights[0].shape[1]
    return (
        far_weight_kernel,
        [*lefts, *rights],
        [((share, width), BF16), ((share, width), F32)],
        [((2 * share, 256), F32)],
    )


def fill_lefts(place, turns, own, cuts, first, buf):
    m = place[0]
    quarter = buf.shape[0] // (4 * turns)
    pair = buf.shape[1]
    lanes = pair_lanes(place, buf)
    for p in range(4):
        rows = slice(p * quarter, (p + 1) * quarter)
        if len(own) == 1:
            from_rows = pl.ds(pl.multiple_of((m ^ p) * quarter, quarter), quarter)
            buf[rows, :] = own[0][from_rows, lanes]
        else:
            buf[rows, :] = own[p][:, lanes]
        for block in range(1, turns):
            at = (4 * block + p) * quarter
            piece = cuts[p][(block - 1) * quarter : block * quarter, first : first + pair]
            buf[at : at + quarter, :] = piece


def both_kernel(turns, place, *refs):
    branch, normed, cuts = refs[0:4], refs[4:5], refs[5:9]
    d_outgate, gated = refs[9], refs[10]
    outgates, gateds = refs[11 : 10 + turns], refs[10 + turns : 9 + 2 * turns]
    sent, kept, buf, res = refs[9 + 2 * turns :]
    length = gated.shape[0]
    pair, half = buf.shape[1], gated.shape[1]
    for own, first, rights, at in (
        (branch, pair, (gated, *gateds), 0),
        (normed, 0, (d_outgate, *outgates), half),
    ):
        fill_lefts(place, turns, own, cuts, first, buf)
        blocks = [
            (buf.at[block * length : (block + 1) * length, :], right, 0, None)
            for block, right in enumerate(rights)
        ]
        pair_sums(blocks, place[2], sent, kept, res, at)


def pre_kernel(turns, place, *refs):
    normed, cuts, rights = refs[0:1], refs[1:5], refs[5 : 5 + turns]
    sent, kept, buf, res = refs[5 + turns :]
    length = rights[0].shape[0]
    fill_lefts(place, turns, normed, cuts, 0, buf)
    blocks = [
        (buf.at[block * length : (block + 1) * length, :], right, 0)
        for block, right in enumerate(rights)
    ]
    pair_sums(blocks, place[2], sent, kept, res)


def zone_weight(body, turns, share, length, width, args):
    return (
        functools.partial(body, turns),
        args,
        [((share, width), BF16), ((share, width), F32)],
        [((turns * length, 2 * share), BF16), ((2 * share, 256), F32)],
    )


def edge_kernel(place, d_pre, last_rows, from_next, keep, out):
    quarter = d_pre.shape[0] // 4
    out[...] = d_pre[...]
    at = pl.multiple_of((place[0] ^ 3) * quarter + quarter - 8, 8)
    out[pl.ds(at, 8), :] = (last_rows[...] + from_next[...] * keep[...]).astype(BF16)


def stack_kernel(place, *refs):
    stack(refs[:-1], refs[-1])


def natural_kernel(row, place, own, side, other_own, other_side, out):
    quarter = out.shape[0] // 4
    for p, ref in enumerate((own, side, other_own, other_side)):
        to = pl.multiple_of((place[0] ^ p) * quarter, quarter)
        out[pl.ds(to, quarter), :] = ref[row : row + quarter, :].astype(F32)


def settle_kernel(place, kept, got, out_0, out_1, out_2):
    at = 0
    for out in (out_0, out_1, out_2):
        width = out.shape[1]
        out[...] = kept[:, at : at + width] + got[:, at : at + width].astype(F32)
        at += width


def low_kernel(place, d_low, normed, pack, first, second, outnorm, squared, out):
    out[0:RANK, :] = dot(d_low[...], normed[...])
    out[RANK:, :] = pack[...]
    out[RANK + 5 : RANK + 6, :] = first[...]
    out[RANK + 6 : RANK + 7, :] = second[...]
    out[RANK + 7 : RANK + 8, 0:DV] = outnorm[...]
    out[RANK + 7 : RANK + 8, DV : 2 * DV] = jnp.broadcast_to(squared[...], (1, DV))


def unpack_kernel(share, place, summed, query_out, key_out, value_out, up_out, bias_out, down_out):
    for row in range(TAPS):
        at = (row % 2) * (2 * DK + DV)
        line = summed[RANK + row // 2 : RANK + 1 + row // 2, :]
        query_out[row : row + 1, :] = line[:, at : at + DK]
        key_out[row : row + 1, :] = line[:, at + DK : at + 2 * DK]
        value_out[row : row + 1, :] = line[:, at + 2 * DK : at + 2 * DK + DV]
    per = D // DK
    for row in range(RANK):
        at = (row % per) * DK
        up_out[row : row + 1, :] = summed[RANK + 2 + row // per : RANK + 3 + row // per, at : at + DK]
    bias_out[...] = summed[RANK + 4 : RANK + 5, 0:DK]
    pair = 2 * share
    both = summed[0:RANK, pl.ds(pl.multiple_of(place[1] * pair, pair), pair)]
    down_out[...] = jnp.where(place[2] == 0, both[:, 0:share], both[:, share:])


COST = {
    "state_kernel": 2.3,
    "output_kernel": 2.0,
    "gate_back_kernel": 2.0,
    "mixer_back_kernel": 4.5,
    "rows_kernel": 2.8,
    "gate_kernel": 5.0,
    "gate_back_kernel_rows": 3.0,
    "far_back_kernel": 4.0,
    "far_weight_kernel": 2.5,
    "both_kernel": 3.0,
    "pre_kernel": 2.0,
    "natural_kernel": 2.0,
}


def on_device(
    block_input,
    first_gain,
    query_weight,
    key_weight,
    value_weight,
    query_conv,
    key_conv,
    value_conv,
    lowrank_down,
    lowrank_up,
    decay_bias,
    outgate_weight,
    outnorm_gain,
    output_weight,
    second_gain,
    gate_weight,
    up_weight,
    down_weight,
    starts,
    valid_mask,
    cotangent,
    teacher,
):
    length = block_input.shape[0]
    quarter, half = length // 4, length // 2
    places = lax.axis_size("seq")
    turns = places // 2
    share = D // places
    pair = 2 * share
    hidden_units = gate_weight.shape[1]
    channels = 2 * DK + DV
    seq, head = lax.axis_index("seq"), lax.axis_index("head")
    mine = (head % 2) * 2 + head // 2
    zone, side = seq // 2, seq % 2
    place = jnp.stack([mine, zone, side]).astype(jnp.int32)
    loss_weight = float(length * places * D // 8)
    row_shape = (quarter, D)
    window_shape = (DK + 16, 2 * DK)
    roomy = 6 if turns <= 4 else 20


    waiting = []

    def run(body, args, outs, scratch=(), vmem=6):
        micros = COST.get(getattr(body, "func", body).__name__, 1.0)
        gate = after(place, *waiting) if waiting else place
        made = call(body, gate, args, outs, scratch, vmem, micros)
        waiting[:] = [made[-1]]
        return made

    def hold(*xs):
        waiting.extend(xs)
        return xs[0] if len(xs) == 1 else xs

    def ready(x):
        return after(x, *waiting)

    def fold(sent, kept):
        got = flip(sent, "head", 1)
        return run(fold_kernel, [kept, got], [(row_shape, F32), (row_shape, BF16)])

    def quarters(own_rows, side_rows):
        return [own_rows, side_rows, flip(own_rows, "head", 1), flip(side_rows, "head", 1)]

    start_row = starts.astype(F32).reshape(1, length)
    input_float = block_input.astype(F32)
    normed = (input_float * root_scale(input_float) * first_gain).astype(BF16)
    pre_k = dot(normed, key_weight).astype(BF16)
    pre_v = dot(normed, value_weight).astype(BF16)
    pre_q = dot(normed, query_weight).astype(BF16)
    last_start, before_last = start_row[0, length - 1], start_row[0, length - 2]
    keep_one = 1.0 - last_start
    tail_keep = jnp.concatenate(
        [jnp.zeros((5,), F32), jnp.stack([keep_one * (1.0 - before_last), keep_one, jnp.ones((), F32)])]
    )
    tails = jnp.concatenate([pre_q[length - 8 :], pre_k[length - 8 :], pre_v[length - 8 :]], axis=1)
    edge = shift(tails * tail_keep[:, None].astype(BF16), "seq", 1)
    taps = jnp.concatenate([query_conv, key_conv, value_conv], axis=1)
    low_rank = dot(normed, lowrank_down).astype(BF16)
    u, v, x, logit, window = run(
        state_kernel,
        [pre_q, pre_k, pre_v, edge, taps, start_row, low_rank, lowrank_up, decay_bias.reshape(1, DK)],
        [
            ((length, channels), F32),
            ((length, DV), BF16),
            ((length, DK), F32),
            ((length, DK), F32),
            (window_shape, BF16),
        ],
        [((length + 8, channels), F32)],
    )

    def carry(window, sign, beside):
        found = None
        step, at = 1, 0
        while step < places:
            last = 2 * step >= places
            got = shift(window, "seq", sign * step)
            got, *_ = beside(at, step, got, window)
            args = [got] + ([] if last else [window]) + ([] if found is None else [found])
            outs = [((DK, DV), BF16)] if last else [(window_shape, BF16), (window_shape, BF16)]
            made = run(functools.partial(carry_kernel, found is None, last), args, outs)
            if not last:
                window, found = made
            step, at = 2 * step, at + 1
        return made[0]

    def finish(blocks):
        while len(blocks) < turns - 1:
            blocks.append(turn(blocks[-1], 1))
        return blocks

    valid_float = valid_mask.astype(F32)
    counts, outgates = [jnp.full((8, 128), jnp.sum(valid_float), F32)], []

    def with_forward(at, step, got, window):
        count = after(counts[-1], window)
        beside = [count + flip(count, "seq", step)]
        if at == 0:
            beside.append(dot(after(normed, window), outgate_weight))
        got, *beside = join(got, *beside)
        counts.append(beside[0])
        outgates.extend(beside[1:])
        return (got,)

    state_in = carry(window, 1, with_forward)
    outgate, valid_count = outgates[0], counts[-1]
    gain_row = outnorm_gain.reshape(1, DV)
    second_row = second_gain.reshape(1, D)
    first_row = first_gain.reshape(1, D)
    valid_row = valid_float.reshape(1, length)
    steps = [("seq", bit) for bit in (1 << p for p in range(16)) if bit < places]
    gated, mixed, scores, sent, kept = run(
        output_kernel,
        [u, v, x, start_row, state_in, outgate, gain_row, output_weight],
        [
            ((length, DV), BF16),
            ((length, DV), F32),
            ((length, length), BF16),
            ((half, D), BF16),
            ((half, D), F32),
        ],
    )

    near, far = fold(sent, kept)
    far, turned = join(far, gated)
    far, gated_1 = join(flip(far, "head", 2), turn(turned, 1))
    hidden, ffn_own = run(
        hidden_kernel, [near, far, block_input, second_row], [(row_shape, F32), (row_shape, BF16)]
    )
    ffn_side, ffn_1 = join(flip(ffn_own, "head", 2), turn(ffn_own, 1))
    ffn_in = quarters(ffn_own, ffn_side)
    activated, gate_in, up_in = run(*gate_up(ffn_in, gate_weight, up_weight))
    sent, kept = run(*rows_times([activated], [(0, 0, hidden_units, down_weight)]))
    near, far = fold(sent, kept)
    far, turned = join(far, ffn_1)
    far, ffn_2 = join(flip(far, "head", 2), turn(turned, 1))
    output_own, d_out, d_ffn_own, squared = run(
        functools.partial(loss_kernel, loss_weight),
        [near, far, hidden, teacher, cotangent, valid_row, valid_count],
        [(row_shape, BF16), (row_shape, F32), (row_shape, BF16), ((1, 1), F32)],
    )
    d_ffn_own, turned, turned_too = join(d_ffn_own, ffn_2, gated_1)
    d_ffn_side, ffn_3, gated_2 = join(
        flip(d_ffn_own, "head", 2), turn(turned, 1), turn(turned_too, 1)
    )
    d_ffn = quarters(d_ffn_own, d_ffn_side)
    d_gate, d_up = run(*gate_back_rows(d_ffn, down_weight, gate_in, up_in))
    ffn_turns = [ffn_own, *finish([ffn_1, ffn_2, ffn_3])]
    (ffn_far,) = run(stack_kernel, ffn_turns[1:], [(((turns - 1) * quarter, D), BF16)])
    sent, kept = run(
        *rows_times(
            [d_gate, d_up],
            [(0, 0, hidden_units, gate_weight), (1, 0, hidden_units, up_weight)],
        )
    )
    near, far = fold(sent, kept)
    far, turned = join(far, d_ffn_own)
    far, d_1 = join(flip(far, "head", 2), turn(turned, 1))
    d_hidden, d_branch_own, second_part, *cuts = run(
        functools.partial(hidden_back_kernel, turns),
        [near, far, hidden, d_out, second_row, normed],
        [(row_shape, F32), (row_shape, BF16), ((1, D), F32)]
        + [((quarter, 2 * pair), BF16)] * (turns - 1),
    )
    d_branch_own, turned, turned_too = join(d_branch_own, d_1, gated_2)
    d_branch_side, d_2, gated_3 = join(
        flip(d_branch_own, "head", 2), turn(turned, 1), turn(turned_too, 1)
    )
    gated_turns = finish([gated_1, gated_2, gated_3])
    d_branch = quarters(d_branch_own, d_branch_side)

    d_outgate, d_mixed, outnorm_part, direct = run(
        gate_back_kernel,
        [*d_branch, output_weight, mixed, outgate, gain_row, u, x, start_row],
        [((length, DV), BF16), ((length, DV), BF16), ((1, DV), F32), (window_shape, BF16)],
        [((length, D), BF16)],
    )
    (d_far,) = run(stack_kernel, [d_1, d_2], [((half, D), BF16)])

    d_turns, d_sides, cuts_got, outgate_turns = [d_ffn_own, d_1, d_2], [d_ffn_side], [], []
    made, grads, sums, held = [], [], {}, {}

    def weigh(name, lefts, rights):
        sums[name] = run(*far_weight(share, lefts, rights))

    def with_back(at, step, got, window):
        if at == 0:
            got, third, sides = join(
                got, turn(after(d_2, window), 1), flip(after(ffn_far, d_branch_side), "head", 2)
            )
            d_turns.append(third)
            held["ffn"] = sides
        elif at == 1:
            sides = flip(after(d_far, window), "head", 2)
            right = turn(after(d_outgate, window), 1)
            made.append(
                run(
                    *far_gate_up(ffn_turns, [ffn_side, held["ffn"]], gate_weight, up_weight, pair),
                    vmem=roomy,
                )
            )
            got, sides, right = join(got, sides, right)
            d_sides.append(sides)
            outgate_turns.append(right)
        elif at == 2:
            side = flip(after(d_turns[3], window), "head", 2)
            other = flip(after(made[0][4], window), "head", 1)
            made.append(run(*gate_up([other], gate_weight, up_weight, pair), vmem=roomy))
            right = turn(after(outgate_turns[-1], made[1][3]), 1)
            got, side, right = join(got, side, right)
            d_sides.append(side)
            outgate_turns.append(right)
            for extra in range(4, turns):
                d_turns.append(turn(d_turns[-1], 1))
                d_sides.append(flip(d_turns[-1], "head", 2))
        return (got,)

    later = carry(direct, -1, with_back)
    d_pre, last_rows, pack, d_low, back_rows = run(
        mixer_back_kernel,
        [
            d_mixed, state_in, later, u, v, x, scores, pre_q, pre_k, pre_v, edge, taps,
            logit, start_row, low_rank, lowrank_up,
        ],
        [
            ((length, channels), BF16),
            ((8, channels), F32),
            ((8, D), F32),
            ((RANK, length), F32),
            ((8, channels), F32),
        ],
        [
            ((length + 8, channels), F32),
            ((length + 8, channels), F32),
            ((16, DK), F32),
            ((length, DK), F32),
        ],
        vmem=7,
    )

    grads.append(
        run(
            *far_back_rows(d_turns, d_sides, down_weight, made[0][1], made[0][2], pair), vmem=roomy
        )
    )
    from_next, d_low_got, right, rows_other = join(
        shift(back_rows, "seq", -1),
        flip(d_low, "head", 1),
        turn(after(outgate_turns[-1], back_rows), 1),
        flip(grads[0][3], "head", 1),
    )
    outgate_turns = finish([*outgate_turns, right])
    hold(from_next)
    (d_pre,) = run(
        edge_kernel, [d_pre, last_rows, from_next, tail_keep[:, None]], [((length, channels), BF16)]
    )

    pre_1 = turn(d_pre, 1)
    cuts_got = [turn(after(cuts[by - 1], d_pre), by) for by in range(1, turns)]
    d_low = d_low + d_low_got
    grads.append(
        run(*gate_back_rows([rows_other], down_weight, made[1][1], made[1][2], pair), vmem=roomy)
    )
    cuts_in = [part[3] for part in made]
    weigh("gate", cuts_in, [grad[0] for grad in grads])
    pre_1, gate_sent, d_low_got, *cuts_got = join(
        pre_1, sums["gate"][0], flip(d_low, "head", 2), *cuts_got
    )

    pre_2 = turn(pre_1, 1)
    gate_got = flip(gate_sent, "seq", 1)
    hold(pre_1)
    sent, kept = run(
        *rows_times(
            [d_outgate, d_pre],
            [
                (0, 0, DV, outgate_weight),
                (1, 0, DK, query_weight),
                (1, DK, DK, key_weight),
                (1, 2 * DK, DV, value_weight),
            ],
        )
    )
    near, far = fold(sent, kept)
    far = flip(far, "head", 2)
    weigh("up", cuts_in, [grad[1] for grad in grads])
    weigh("down", [grad[2] for grad in grads], [part[0] for part in made])
    (cuts_near,) = run(stack_kernel, cuts_got, [(((turns - 1) * quarter, 2 * pair), BF16)])
    cuts_side = flip(cuts_near, "head", 2)
    grad_own, first_part, d_lowrank = run(
        input_back_kernel,
        [near, far, block_input, d_hidden, first_row, d_low, d_low_got, lowrank_down.T],
        [(row_shape, BF16), ((1, D), F32), ((RANK, length), BF16)],
    )
    (small,) = run(
        low_kernel,
        [d_lowrank, normed, pack, first_part, second_part, outnorm_part, squared],
        [((RANK + 8, D), F32)],
    )
    (rows_both,) = run(stack_kernel, [grad_own, output_own], [((half, D), BF16)])
    pre_2, gate_got, small, rows_both, up_sent, down_sent, cuts_near, cuts_side = join(
        pre_2, gate_got, small, rows_both, sums["up"][0], sums["down"][0], cuts_near, cuts_side
    )

    pre_3 = turn(pre_2, 1)
    cuts_far = quarters(cuts_near, cuts_side)
    shared = total(small[RANK + 5 :], [("head", 1), ("head", 2)])
    up_got = flip(up_sent, "seq", 1)
    rows_side = flip(rows_both, "head", 2)
    sum_both = run(
        *zone_weight(
            both_kernel, turns, share, length, 2 * DV,
            [*d_branch, normed, *cuts_far, d_outgate, gated, *outgate_turns, *gated_turns],
        )
    )
    pre_3, up_got, rows_side, shared, both_sent, rows_both, down_sent = join(
        pre_3, up_got, rows_side, shared, sum_both[0], rows_both, down_sent
    )
    small = jnp.concatenate([small[: RANK + 5], shared], axis=0)
    small = total(after(small, pre_3), steps[:1])
    down_got, both_got = flip(down_sent, "seq", 1), flip(both_sent, "seq", 1)
    sum_pre = run(
        *zone_weight(
            pre_kernel, turns, share, length, channels,
            [normed, *cuts_far, d_pre, *finish([pre_1, pre_2, pre_3])],
        )
    )
    pre_got = flip(sum_pre[0], "seq", 1)
    small = total(after(small, sum_pre[0]), steps[1:])
    shared = small[RANK + 5 :]
    grad_query, grad_key, grad_value = run(
        settle_kernel, [sum_pre[1], pre_got],
        [((share, DK), F32), ((share, DK), F32), ((share, DV), F32)],
    )
    both_other, side_other = flip(rows_both, "head", 1), flip(rows_side, "head", 1)
    (grad_input,) = run(
        functools.partial(natural_kernel, 0),
        [rows_both, rows_side, both_other, side_other],
        [((length, D), F32)],
    )
    (block_output,) = run(
        functools.partial(natural_kernel, quarter),
        [rows_both, rows_side, both_other, side_other],
        [((length, D), F32)],
    )
    grad_gate, grad_up, grad_down, grad_both = (
        after(kept, sum_pre[0]) + got.astype(F32)
        for got, kept in (
            (gate_got, sums["gate"][1]),
            (up_got, sums["up"][1]),
            (down_got, sums["down"][1]),
            (both_got, sum_both[1]),
        )
    )
    grad_output, grad_outgate = grad_both[:, :DV], grad_both[:, DV:]
    apart = small
    taps_query, taps_key, taps_value, grad_lowrank_up, bias_row, down_row = run(
        functools.partial(unpack_kernel, share),
        [apart],
        [
            ((TAPS, DK), F32),
            ((TAPS, DK), F32),
            ((TAPS, DV), F32),
            ((RANK, DK), F32),
            ((1, DK), F32),
            ((RANK, share), F32),
        ],
    )
    distill = shared[2, DV] / (valid_count[0, 0] * D)
    return (
        block_output,
        distill,
        grad_input,
        shared[0],
        grad_query,
        grad_key,
        grad_value,
        taps_query,
        taps_key,
        taps_value,
        down_row.T,
        grad_lowrank_up,
        bias_row.reshape(DK),
        grad_outgate,
        shared[2, :DV],
        grad_output,
        shared[1],
        grad_gate,
        grad_up,
        grad_down,
    )


def solution(mesh):
    rows, cols, whole = P("seq", None), P(None, "head"), P()
    in_specs = (
        rows, whole, cols, cols, cols, cols, cols, cols, whole, cols, P("head"), cols, whole, cols,
        whole, cols, cols, cols, P("seq"), P("seq"), rows, rows,
    )
    tiles = P("seq", "head")
    out_specs = (
        rows, whole, rows, whole, tiles, tiles, tiles, cols, cols, cols, rows, cols, P("head"), tiles,
        whole, tiles, whole, tiles, tiles, tiles,
    )
    return jax.shard_map(
        on_device, mesh=mesh, in_specs=in_specs, out_specs=out_specs, check_vma=False
    )
```

```python
import functools

import functools

import jax
import jax.numpy as jnp
from jax import lax
from jax.experimental import pallas as pl
from jax.experimental.pallas import tpu as pltpu
from jax.sharding import PartitionSpec as P

D = 2048
DK = 256
DV = 512
RANK = 16
TAPS = 4
BLOCK = 64
EPSILON = 1e-05
HIGHEST = lax.Precision.HIGHEST
F32 = jnp.float32
BF16 = jnp.bfloat16
MIB = 1024 * 1024


def contract_rows(left, right):
    return lax.dot_general(left, right, (((0,), (0,)), ((), ())), preferred_element_type=F32)


def contract_cols(left, right):
    return lax.dot_general(left, right, (((1,), (1,)), ((), ())), preferred_element_type=F32)


def dot(left, right, precision=None):
    return lax.dot_general(
        left, right, (((1,), (0,)), ((), ())), precision=precision, preferred_element_type=F32
    )


def root_scale(v):
    return lax.rsqrt(jnp.mean(v * v, axis=-1, keepdims=True) + EPSILON)


def norm_backward(v, scale, gain, upstream):
    scaled_up = upstream * gain
    return scale * scaled_up - v * scale * scale * scale * jnp.mean(
        scaled_up * v, axis=-1, keepdims=True
    )


def flip(x, axis, bit):
    n = lax.axis_size(axis)
    return lax.ppermute(x, axis, [(i, i ^ bit) for i in range(n)])


def shift(x, axis, by):
    n = lax.axis_size(axis)
    return lax.ppermute(x, axis, [(i, i + by) for i in range(n) if 0 <= i + by < n])


def turn(x, by):
    n = lax.axis_size("seq")
    return lax.ppermute(x, "seq", [(i, (i + 2 * by) % n) for i in range(n)])


def after(x, *others):
    return lax.optimization_barrier((x, *others))[0]


def join(*xs):
    return lax.optimization_barrier(xs)


def total(x, steps, kind=F32):
    for axis, bit in steps:
        if kind != F32:
            x = lax.reduce_precision(x, 8, 7)
        x = x + flip(x.astype(kind), axis, bit).astype(F32)
    return x


def grids(n):
    return (
        lax.broadcasted_iota(jnp.int32, (n, n), 0),
        lax.broadcasted_iota(jnp.int32, (n, n), 1),
    )


def column(row, rows, cols, back):
    return jnp.sum(jnp.where(cols == rows - back, row, 0.0), axis=1, keepdims=True)


def tap_masks(start_row, rows, cols):
    here, one, two = (column(start_row, rows, cols, back) for back in range(3))
    first = 1.0 - here
    second = first * (1.0 - one)
    return here, (first, second, second * (1.0 - two))


def segments(start_row, start_col, rows, cols):
    seg_col = jnp.sum(jnp.where(cols <= rows, start_row, 0.0), axis=1, keepdims=True)
    seg_row = jnp.sum(jnp.where(rows <= cols, start_col, 0.0), axis=0, keepdims=True)
    return seg_col, seg_row, jnp.sum(start_row)


def block_middles(x):
    n = x.shape[0] // BLOCK
    mids = []
    for b in range(n):
        last = x[(b + 1) * BLOCK - 1 : (b + 1) * BLOCK]
        before = x[b * BLOCK - 1 : b * BLOCK] if b else jnp.zeros_like(last)
        mids.append(0.5 * (before + last))
    return mids


def spread(mids):
    return jnp.concatenate(
        [jnp.broadcast_to(mid, (BLOCK, mid.shape[1])) for mid in mids], axis=0
    )


def state_kernel(
    place, pre_q, pre_k, pre_v, edge, taps, start_row, low_rank, lowrank_up, bias,
    u_out, v_out, x_out, logit_out, state_out, ext,
):
    n = pre_q.shape[0]
    rows, cols = grids(n)
    sr = start_row[...]
    start_col, masks = tap_masks(sr, rows, cols)
    seg_col, _, seg_last = segments(sr, start_col, rows, cols)
    ext[0:8, :] = edge[...].astype(F32)
    ext[8:, 0:DK] = pre_q[...].astype(F32)
    ext[8:, DK : 2 * DK] = pre_k[...].astype(F32)
    ext[8:, 2 * DK :] = pre_v[...].astype(F32)
    for part in range(4):
        lanes = slice(part * DK, (part + 1) * DK)
        u = ext[8 : 8 + n, lanes] * taps[3:4, lanes]
        for back in range(1, TAPS):
            u = u + ext[8 - back : 8 - back + n, lanes] * taps[3 - back : 4 - back, lanes] * masks[
                back - 1
            ]
        u_out[:, lanes] = u
        if part >= 2:
            v_out[:, (part - 2) * DK : (part - 1) * DK] = (u * jax.nn.sigmoid(u)).astype(BF16)
    logit = dot(low_rank[...], lowrank_up[...]) + bias[...]
    logit_out[...] = logit
    decays = (jnp.minimum(logit, 0.0) - jnp.log1p(jnp.exp(-jnp.abs(logit)))) * (1.0 / 16.0)
    x = dot((cols <= rows).astype(F32), decays, HIGHEST)
    x_out[...] = x
    u = u_out[:, DK : 2 * DK]
    keys = u * jax.nn.sigmoid(u)
    tail = (seg_col == seg_last).astype(F32)
    final = x[n - 1 : n]
    closing = (keys * jnp.exp(final - x) * tail).astype(BF16)
    put_decay(
        state_out,
        contract_rows(closing, v_out[...]).astype(BF16),
        jnp.exp(final) * (seg_last == 0.0).astype(F32),
    )


def local_scores(q, k, x):
    n = x.shape[0] // BLOCK
    mids = block_middles(x)
    mid = spread(mids)
    grow, shrink = jnp.exp(x - mid), jnp.exp(mid - x)
    rising, falling = q * grow, (k * shrink).astype(BF16)
    lifted, scales = [], []
    for j in range(n):
        pieces = [jnp.exp(mids[i] - mids[j]) for i in range(j, n)]
        scale = spread(pieces)
        scales.append(scale)
        lifted.append((rising[j * BLOCK :] * scale).astype(BF16))
    return grow, shrink, lifted, scales, falling


def output_kernel(
    place, u_qk, v, x_in, start_row, state_in, outgate, gain, weight,
    gated_out, mixed_out, scores_out, sent_out, kept_out,
):
    n = x_in.shape[0]
    blocks = n // BLOCK
    rows, cols = grids(n)
    sr = start_row[...]
    start_col = column(sr, rows, cols, 0)
    seg_col, seg_row, _ = segments(sr, start_col, rows, cols)
    allowed = (cols <= rows) & (seg_col == seg_row)
    alive = (seg_col == 0.0).astype(F32)
    x = x_in[...]
    uq = u_qk[:, 0:DK]
    uk = u_qk[:, DK : 2 * DK]
    q = uq * jax.nn.sigmoid(uq) * DK**-0.5
    k = uk * jax.nn.sigmoid(uk)
    _, _, lifted, _, falling = local_scores(q, k, x)
    scores_out[...] = jnp.zeros_like(scores_out)
    for j in range(blocks):
        lo, hi = j * BLOCK, (j + 1) * BLOCK
        s = contract_cols(lifted[j], falling[lo:hi])
        scores_out[lo:, lo:hi] = jnp.where(allowed[lo:, lo:hi], s, 0.0).astype(BF16)
    carried = (q * jnp.exp(x) * alive).astype(BF16)
    out = dot(scores_out[...], v[...]) + dot(carried, state_in[...])
    mixed_out[...] = out
    og = outgate[...]
    gated = (out * root_scale(out) * gain[...] * (og * jax.nn.sigmoid(og))).astype(BF16)
    m = place[0]
    for b in range(blocks):
        at = pl.multiple_of((m ^ b) * BLOCK, BLOCK)
        gated_out[pl.ds(at, BLOCK), :] = gated[b * BLOCK : (b + 1) * BLOCK]
    half = n // 2
    for part in range(4):
        lanes = slice(part * DV, (part + 1) * DV)
        branch = contract_cols(gated_out[...], weight[lanes, :])
        kept_out[:, lanes] = branch[0:half]
        sent_out[:, lanes] = branch[half:].astype(BF16)


def gate_back_kernel(
    place, branch_0, branch_1, branch_2, branch_3, weight, mixed, outgate, gain, u_in, x_in,
    start_row, d_outgate_out, d_mixed_out, gain_out, direct_out, order,
):
    n = x_in.shape[0]
    blocks = n // BLOCK
    m = place[0]
    for p, piece in enumerate((branch_0, branch_1, branch_2, branch_3)):
        at = pl.multiple_of((m ^ p) * BLOCK, BLOCK)
        order[pl.ds(at, BLOCK), :] = piece[...]
    up = dot(order[...], weight[...])
    og = outgate[...]
    sig = jax.nn.sigmoid(og)
    out = mixed[...]
    scale = root_scale(out)
    g = gain[...]
    d_outgate = (up * (out * scale * g) * sig * (1.0 + og * (1.0 - sig))).astype(BF16)
    for b in range(blocks):
        at = pl.multiple_of((m ^ b) * BLOCK, BLOCK)
        d_outgate_out[pl.ds(at, BLOCK), :] = d_outgate[b * BLOCK : (b + 1) * BLOCK]
    d_norm = up * (og * sig)
    gain_out[...] = jnp.sum(d_norm * out * scale, axis=0, keepdims=True)
    d_mixed = norm_backward(out, scale, g, d_norm).astype(BF16)
    d_mixed_out[...] = d_mixed
    rows, cols = grids(n)
    sr = start_row[...]
    seg_col = jnp.sum(jnp.where(cols <= rows, sr, 0.0), axis=1, keepdims=True)
    alive = (seg_col == 0.0).astype(F32)
    uq = u_in[:, 0:DK]
    x = x_in[...]
    carried = (uq * jax.nn.sigmoid(uq) * DK**-0.5 * jnp.exp(x) * alive).astype(BF16)
    put_decay(
        direct_out,
        contract_rows(carried, d_mixed).astype(BF16),
        jnp.exp(x[n - 1 : n]) * (jnp.sum(sr) == 0.0).astype(F32),
    )


def mixer_back_kernel(
    place, d_mixed, state_in, later, u_in, v, x_in, scores, pre_q, pre_k, pre_v, edge, taps,
    logit, start_row, low_rank, lowrank_up,
    d_pre_out, last_rows_out, pack_out, d_low_out, back_rows_out,
    ext, du_ext, small, dx_buf,
):
    n = x_in.shape[0]
    blocks = n // BLOCK
    m = place[0]
    rows, cols = grids(n)
    sr = start_row[...]
    start_col, masks = tap_masks(sr, rows, cols)
    seg_col, seg_row, seg_last = segments(sr, start_col, rows, cols)
    allowed = (cols <= rows) & (seg_col == seg_row)
    alive = (seg_col == 0.0).astype(F32)
    tail = (seg_col == seg_last).astype(F32)
    x = x_in[...]
    uq = u_in[:, 0:DK]
    uk = u_in[:, DK : 2 * DK]
    sq, sk = jax.nn.sigmoid(uq), jax.nn.sigmoid(uk)
    q = uq * sq * DK**-0.5
    k = uk * sk
    grow, shrink, lifted, scales, falling = local_scores(q, k, x)
    dm = d_mixed[...]
    later_b = later[...]
    later_f = later_b.astype(F32)
    state_f = state_in[...].astype(F32)
    d_scores = jnp.where(allowed, contract_cols(dm, v[...]), 0.0).astype(BF16)
    final = x[n - 1 : n]
    leaving = jnp.exp(final - x) * tail
    closing = (k * leaving).astype(BF16)
    d_closing = contract_cols(v[...], later_b)
    entering = jnp.exp(x) * alive
    d_carried = contract_cols(dm, state_in[...])
    dq = d_carried * entering
    dk = d_closing * leaving
    closed = d_closing * closing.astype(F32)
    dx_buf[...] = d_carried * (q * entering) - closed
    through = jnp.sum(later_f * state_f, axis=1, keepdims=True)
    through_row = jnp.sum(jnp.where(rows == cols, through, 0.0), axis=0, keepdims=True)
    at_last = jnp.sum(closed, axis=0, keepdims=True) + through_row * jnp.exp(final) * (
        seg_last == 0.0
    ).astype(F32)
    dx_buf[n - 1 : n, :] = dx_buf[n - 1 : n, :] + at_last
    dq_parts = [dq[b * BLOCK : (b + 1) * BLOCK] for b in range(blocks)]
    dk_parts = []
    for j in range(blocks):
        lo, hi = j * BLOCK, (j + 1) * BLOCK
        ds = d_scores[lo:, lo:hi]
        d_lift = dot(ds, falling[lo:hi])
        d_fall = contract_rows(ds, lifted[j])
        dx_buf[lo:, :] = dx_buf[lo:, :] + d_lift * lifted[j].astype(F32)
        dx_buf[lo:hi, :] = dx_buf[lo:hi, :] - d_fall * falling[lo:hi].astype(F32)
        d_rise = d_lift * scales[j] * grow[lo:]
        for b in range(j, blocks):
            dq_parts[b] = dq_parts[b] + d_rise[(b - j) * BLOCK : (b - j + 1) * BLOCK]
        dk_parts.append(dk[lo:hi] + d_fall * shrink[lo:hi])
    dq = jnp.concatenate(dq_parts, axis=0)
    dk = jnp.concatenate(dk_parts, axis=0)
    d_decays = dot((cols >= rows).astype(F32), dx_buf[...], HIGHEST)
    d_logit = (d_decays * jax.nn.sigmoid(-logit[...]) * (1.0 / 16.0)).astype(BF16)
    pack_out[...] = jnp.zeros_like(pack_out)
    pack_out[4:5, 0:DK] = jnp.sum(d_logit.astype(F32), axis=0, keepdims=True)
    d_up = contract_rows(low_rank[...], d_logit)
    per = pack_out.shape[1] // DK
    for row in range(RANK):
        at = (row % per) * DK
        pack_out[2 + row // per : 3 + row // per, at : at + DK] = d_up[row : row + 1]
    d_low_out[...] = contract_cols(lowrank_up[...], d_logit)

    ext[0:8, :] = edge[...].astype(F32)
    ext[8:, 0:DK] = pre_q[...].astype(F32)
    ext[8:, DK : 2 * DK] = pre_k[...].astype(F32)
    ext[8:, 2 * DK :] = pre_v[...].astype(F32)
    du_ext[n:, :] = jnp.zeros((8, du_ext.shape[1]), F32)
    du_ext[0:n, 0:DK] = dq * (DK**-0.5) * (sq * (1.0 + uq * (1.0 - sq)))
    du_ext[0:n, DK : 2 * DK] = dk * (sk * (1.0 + uk * (1.0 - sk)))
    dv = contract_rows(scores[...], dm) + dot(closing, later_b)
    for half in range(2):
        uv = u_in[:, (2 + half) * DK : (3 + half) * DK]
        sv = jax.nn.sigmoid(uv)
        du_ext[0:n, (2 + half) * DK : (3 + half) * DK] = dv[:, half * DK : (half + 1) * DK] * (
            sv * (1.0 + uv * (1.0 - sv))
        )
    ahead = []
    for back in range(1, TAPS):
        mask_row = jnp.sum(jnp.where(rows == cols, masks[back - 1], 0.0), axis=0, keepdims=True)
        ahead.append(column(mask_row, rows, cols, -back))
    for part in range(4):
        lanes = slice(part * DK, (part + 1) * DK)
        du = du_ext[0:n, lanes]
        d_pre = du * taps[3:4, lanes]
        back_rows = jnp.zeros((8, DK), F32)
        wide = du_ext.shape[1]
        pack_out[1:2, wide + part * DK : wide + (part + 1) * DK] = jnp.sum(
            du * ext[8 : 8 + n, lanes], axis=0, keepdims=True
        )
        for back in range(1, TAPS):
            weight = taps[3 - back : 4 - back, lanes]
            d_pre = d_pre + du_ext[back : back + n, lanes] * weight * ahead[back - 1]
            masked = du * masks[back - 1]
            row, at = (3 - back) // 2, (3 - back) % 2 * wide + part * DK
            pack_out[row : row + 1, at : at + DK] = jnp.sum(
                masked * ext[8 - back : 8 - back + n, lanes], axis=0, keepdims=True
            )
            small[0:8, :] = jnp.zeros((8, DK), F32)
            small[8:16, :] = masked[0:8]
            back_rows = back_rows + small[back : back + 8, :] * weight
        back_rows_out[:, lanes] = back_rows
        last_rows_out[:, lanes] = d_pre[n - 8 :]
        rounded = d_pre.astype(BF16)
        for b in range(blocks):
            at = pl.multiple_of((m ^ b) * BLOCK, BLOCK)
            d_pre_out[pl.ds(at, BLOCK), lanes] = rounded[b * BLOCK : (b + 1) * BLOCK]


def whole_spec():
    return pl.BlockSpec(memory_space=pltpu.VMEM)


def call(body, place, args, outs, scratch=(), vmem=6, micros=1.0):
    return pl.pallas_call(
        body,
        out_shape=[jax.ShapeDtypeStruct(shape, kind) for shape, kind in outs],
        in_specs=[pl.BlockSpec(memory_space=pltpu.SMEM)] + [whole_spec() for _ in args],
        out_specs=[whole_spec() for _ in outs],
        scratch_shapes=[pltpu.VMEM(shape, kind) for shape, kind in scratch],
        compiler_params=pltpu.CompilerParams(vmem_limit_bytes=vmem * MIB),
        cost_estimate=pl.CostEstimate(
            flops=int(micros * 1e9), bytes_accessed=int(micros * 3e6), transcendentals=0
        ),
    )(place, *args)


def spans(width, tile):
    return [slice(at, min(at + tile, width)) for at in range(0, width, tile)]


def fold_kernel(place, kept, got, near_out, far_out):
    quarter = near_out.shape[0]
    near_out[...] = kept[0:quarter] + got[0:quarter].astype(F32)
    far_out[...] = (kept[quarter:] + got[quarter:].astype(F32)).astype(BF16)


def own_rows(place, ref, quarter):
    return ref[pl.ds(pl.multiple_of(place[0] * quarter, quarter), quarter), :]


def hidden_kernel(place, kept, got, rows, gain, hidden_out, ffn_out):
    hidden = own_rows(place, rows, kept.shape[0]).astype(F32) + (kept[...] + got[...].astype(F32))
    hidden_out[...] = hidden
    ffn_out[...] = (hidden * root_scale(hidden) * gain[...]).astype(BF16)


def loss_kernel(
    weight, place, kept, got, hidden, teacher, cotangent, valid, count,
    output_out, d_out_out, d_ffn_out, squared_out,
):
    quarter = kept.shape[0]
    output = hidden[...] + (kept[...] + got[...].astype(F32))
    output_out[...] = output.astype(BF16)
    mismatch = output - own_rows(place, teacher, quarter).astype(F32)
    length = valid.shape[1]
    rows = lax.broadcasted_iota(jnp.int32, (quarter, length), 0) + place[0] * quarter
    cols = lax.broadcasted_iota(jnp.int32, (quarter, length), 1)
    keep = jnp.sum(jnp.where(rows == cols, valid[...], 0.0), axis=1, keepdims=True)
    squares = jnp.sum(keep * mismatch * mismatch, axis=0, keepdims=True)
    squared_out[...] = jnp.sum(squares, axis=1, keepdims=True)
    scaled = keep * (2.0 * weight) * mismatch / (count[0:1, 0:1] * D)
    d_out = own_rows(place, cotangent, quarter).astype(F32) + scaled
    d_out_out[...] = d_out
    d_ffn_out[...] = d_out.astype(BF16)


def hidden_back_kernel(
    turns, place, kept, got, hidden, d_out, gain, normed, d_hidden_out, d_branch_out, gain_out, *cuts
):
    d_norm = kept[...] + got[...].astype(F32)
    h = hidden[...]
    scale = root_scale(h)
    gain_out[...] = jnp.sum(d_norm * h * scale, axis=0, keepdims=True)
    d_hidden = d_out[...] + norm_backward(h, scale, gain[...], d_norm)
    d_hidden_out[...] = d_hidden
    d_branch_out[...] = d_hidden.astype(BF16)
    quarter = kept.shape[0]
    rows = pl.ds(pl.multiple_of(place[0] * quarter, quarter), quarter)
    for by, cut in enumerate(cuts, 1):
        pair = cut.shape[1] // 2
        target = place[1] + by
        target = jnp.where(target >= turns, target - turns, target)
        lanes = pl.ds(pl.multiple_of(target * pair, pair), pair)
        cut[:, 0:pair] = normed[rows, lanes]
        cut[:, pair:] = d_branch_out[:, lanes]


def input_back_kernel(
    place, kept, got, rows, d_hidden, gain, d_low, d_low_got, down_turned,
    grad_out, gain_out, d_low_out,
):
    quarter, length = kept.shape[0], d_low.shape[1]
    d_lowrank = (d_low[...] + d_low_got[...]).astype(BF16)
    d_low_out[...] = d_lowrank
    here = lax.broadcasted_iota(jnp.int32, (quarter, length), 0) + place[0] * quarter
    tokens = lax.broadcasted_iota(jnp.int32, (quarter, length), 1)
    own_low = contract_cols((here == tokens).astype(BF16), d_lowrank).astype(BF16)
    d_norm = (kept[...] + got[...].astype(F32)) + dot(own_low, down_turned[...])
    v = own_rows(place, rows, quarter).astype(F32)
    scale = root_scale(v)
    gain_out[...] = jnp.sum(d_norm * v * scale, axis=0, keepdims=True)
    grad_out[...] = (d_hidden[...] + norm_backward(v, scale, gain[...], d_norm)).astype(BF16)


def carry_kernel(first, last, place, got, *refs):
    refs = list(refs)
    window = None if last else refs.pop(0)
    found = None if first else refs.pop(0)
    n = DK
    rows, cols = grids(n)

    def as_column(row):
        return jnp.sum(jnp.where(rows == cols, row, 0.0), axis=1, keepdims=True)

    def decay_of(ref):
        both = ref[n : n + 1, :].astype(F32)
        return both[:, 0:n] + both[:, n : 2 * n]

    arrived = got[0:n, :].astype(F32)
    if first:
        merged = arrived
        found_decay = decay_of(got)
    else:
        own = decay_of(found)
        merged = as_column(own) * arrived + found[0:n, :].astype(F32)
        found_decay = own * decay_of(got)
    if last:
        refs.pop(0)[...] = merged.astype(BF16)
        return
    window_decay = decay_of(window)
    state = as_column(window_decay) * arrived + window[0:n, :].astype(F32)
    put_decay(refs.pop(0), state.astype(BF16), window_decay * decay_of(got))
    put_decay(refs.pop(0), merged.astype(BF16), found_decay)


def put_decay(ref, state, decay):
    n = DK
    ref[0:n, :] = state
    high = decay.astype(BF16)
    low = (decay - high.astype(F32)).astype(BF16)
    row = jnp.concatenate([high, low], axis=1)
    ref[n:, :] = jnp.broadcast_to(row, (ref.shape[0] - n, 2 * n))


def rows_kernel(count, widths, place, *refs):
    lefts, rights = refs[:count], refs[count : count + len(widths)]
    sent, kept = refs[count + len(widths) :]
    half = sent.shape[0]
    for lanes in spans(kept.shape[1], 1024):
        acc = None
        for (left, at, width), right in zip(widths, rights):
            term = contract_cols(lefts[left][:, at : at + width], right[lanes, :])
            acc = term if acc is None else acc + term
        kept[:, lanes] = acc[0:half]
        sent[:, lanes] = acc[half:].astype(BF16)


def rows_times(lefts, pairs):
    half = lefts[0].shape[0] // 2
    widths = [pair[:3] for pair in pairs]
    return (
        functools.partial(rows_kernel, len(lefts), widths),
        [*lefts, *(pair[3] for pair in pairs)],
        [((half, D), BF16), ((half, D), F32)],
    )


def stack(pieces, buf):
    at = 0
    for piece in pieces:
        buf[at : at + piece.shape[0], :] = piece[...]
        at += piece.shape[0]


def pair_lanes(place, cut_out):
    pair = cut_out.shape[1]
    return pl.ds(pl.multiple_of(place[1] * pair, pair), pair)


def stacked(pieces, rest):
    if len(pieces) == 1:
        return pieces[0], rest
    stack(pieces, rest[-1])
    return rest[-1], rest[:-1]


def gate_parts(buf, gate_w, up_w, act_out, gate_out, up_out):
    for rows in spans(buf.shape[0], 512):
        for lanes in spans(gate_w.shape[1], 256):
            gate, up = dot(buf[rows, :], gate_w[:, lanes]), dot(buf[rows, :], up_w[:, lanes])
            sig = jax.nn.sigmoid(gate)
            swish = gate * sig
            act_out[rows, lanes] = (swish * up).astype(BF16)
            gate_out[rows, lanes] = (up * sig * (1.0 + gate * (1.0 - sig))).astype(BF16)
            up_out[rows, lanes] = swish.astype(BF16)


def gate_back_parts(buf, down_w, gate_in, up_in, d_gate_out, d_up_out):
    for rows in spans(buf.shape[0], 512):
        for lanes in spans(down_w.shape[1], 256):
            d_act = dot(buf[rows, :], down_w[:, lanes])
            d_gate_out[rows, lanes] = (d_act * gate_in[rows, lanes].astype(F32)).astype(BF16)
            d_up_out[rows, lanes] = (d_act * up_in[rows, lanes].astype(F32)).astype(BF16)


def gate_kernel(count, place, *refs):
    buf, rest = stacked(refs[:count], refs[count:])
    for cut_out in rest[5:]:
        cut_out[...] = buf[:, pair_lanes(place, cut_out)]
    gate_parts(buf, *rest[:5])


def gate_up(pieces, gate_weight, up_weight, pair=0):
    length = sum(p.shape[0] for p in pieces)
    width = gate_weight.shape[1]
    return (
        functools.partial(gate_kernel, len(pieces)),
        [*pieces, gate_weight, up_weight],
        [((length, width), BF16)] * 3 + [((length, pair), BF16)] * (pair > 0),
        [((length, D), BF16)] * (len(pieces) > 1),
    )


def gate_back_kernel_rows(count, place, *refs):
    buf, rest = stacked(refs[:count], refs[count:])
    for cut_out in rest[5:]:
        cut_out[...] = buf[:, pair_lanes(place, cut_out)]
    gate_back_parts(buf, *rest[:5])


def gate_back_rows(pieces, down_weight, gate_in, up_in, pair=0):
    length, width = gate_in.shape
    return (
        functools.partial(gate_back_kernel_rows, len(pieces)),
        [*pieces, down_weight, gate_in, up_in],
        [((length, width), BF16)] * 2 + [((length, pair), BF16)] * (pair > 0),
        [((length, D), BF16)] * (len(pieces) > 1),
    )


def zone_rows(turns, place, refs, buf):
    owns, sides = refs[:turns], []
    taken = turns
    quarter = buf.shape[0] // (2 * turns)
    while len(sides) < turns:
        ref = refs[taken]
        sides += [(ref, at) for at in range(0, ref.shape[0], quarter)]
        taken += 1
    zone = place[1]
    for by in range(turns):
        source = jnp.where(zone < by, zone - by + turns, zone - by)
        at = pl.multiple_of(2 * source * quarter, quarter)
        buf[pl.ds(at, quarter), :] = owns[by][:, 0:D]
        ref, row = sides[by]
        buf[pl.ds(at + quarter, quarter), :] = ref[row : row + quarter, :]
    return refs[taken:]


def far_gate_kernel(turns, place, *refs):
    buf = refs[-1]
    gate_w, up_w, *outs = zone_rows(turns, place, refs[:-1], buf)
    outs[3][...] = buf[:, pair_lanes(place, outs[3])]
    gate_parts(buf, gate_w, up_w, *outs[:3])


def far_gate_up(owns, sides, gate_weight, up_weight, pair):
    length, width = 2 * len(owns) * owns[0].shape[0], gate_weight.shape[1]
    return (
        functools.partial(far_gate_kernel, len(owns)),
        [*owns, *sides, gate_weight, up_weight],
        [((length, width), BF16)] * 3 + [((length, pair), BF16), ((length, D), BF16)],
    )


def far_back_kernel(turns, place, *refs):
    buf = refs[-1]
    down_w, gate_in, up_in, d_gate_out, d_up_out, cut_out = zone_rows(turns, place, refs[:-1], buf)
    cut_out[...] = buf[:, pair_lanes(place, cut_out)]
    gate_back_parts(buf, down_w, gate_in, up_in, d_gate_out, d_up_out)


def far_back_rows(owns, sides, down_weight, gate_in, up_in, pair):
    length, width = gate_in.shape
    return (
        functools.partial(far_back_kernel, len(owns)),
        [*owns, *sides, down_weight, gate_in, up_in],
        [((length, width), BF16)] * 2 + [((length, pair), BF16), ((length, D), BF16)],
    )


def pair_sums(blocks, side, sent, kept, res, at=0):
    share = kept.shape[0]
    width_all = kept.shape[1] // (2 if at or len(blocks[0]) == 4 else 1)
    for cols in spans(width_all, 256):
        acc = None
        for left, right, first, *_ in blocks:
            term = contract_rows(left[...], right[:, first + cols.start : first + cols.stop])
            acc = term if acc is None else acc + term
        width = cols.stop - cols.start
        out = slice(at + cols.start, at + cols.stop)
        res[:, 0:width] = acc
        sent[:, out] = res[
            pl.ds(pl.multiple_of((1 - side) * share, share), share), 0:width
        ].astype(BF16)
        kept[:, out] = res[pl.ds(pl.multiple_of(side * share, share), share), 0:width]


def far_weight_kernel(place, *refs):
    sent, kept, res = refs[-3:]
    count = (len(refs) - 3) // 2
    blocks = [(left, right, 0) for left, right in zip(refs[:count], refs[count:-3])]
    pair_sums(blocks, place[2], sent, kept, res)


def far_weight(share, lefts, rights):
    width = rights[0].shape[1]
    return (
        far_weight_kernel,
        [*lefts, *rights],
        [((share, width), BF16), ((share, width), F32)],
        [((2 * share, 256), F32)],
    )


def fill_lefts(place, turns, own, cuts, first, buf):
    m = place[0]
    quarter = buf.shape[0] // (4 * turns)
    pair = buf.shape[1]
    lanes = pair_lanes(place, buf)
    for p in range(4):
        rows = slice(p * quarter, (p + 1) * quarter)
        if len(own) == 1:
            from_rows = pl.ds(pl.multiple_of((m ^ p) * quarter, quarter), quarter)
            buf[rows, :] = own[0][from_rows, lanes]
        else:
            buf[rows, :] = own[p][:, lanes]
        for block in range(1, turns):
            at = (4 * block + p) * quarter
            piece = cuts[p][(block - 1) * quarter : block * quarter, first : first + pair]
            buf[at : at + quarter, :] = piece


def both_kernel(turns, place, *refs):
    branch, normed, cuts = refs[0:4], refs[4:5], refs[5:9]
    d_outgate, gated = refs[9], refs[10]
    outgates, gateds = refs[11 : 10 + turns], refs[10 + turns : 9 + 2 * turns]
    sent, kept, buf, res = refs[9 + 2 * turns :]
    length = gated.shape[0]
    pair, half = buf.shape[1], gated.shape[1]
    for own, first, rights, at in (
        (branch, pair, (gated, *gateds), 0),
        (normed, 0, (d_outgate, *outgates), half),
    ):
        fill_lefts(place, turns, own, cuts, first, buf)
        blocks = [
            (buf.at[block * length : (block + 1) * length, :], right, 0, None)
            for block, right in enumerate(rights)
        ]
        pair_sums(blocks, place[2], sent, kept, res, at)


def pre_kernel(turns, place, *refs):
    normed, cuts, rights = refs[0:1], refs[1:5], refs[5 : 5 + turns]
    sent, kept, buf, res = refs[5 + turns :]
    length = rights[0].shape[0]
    fill_lefts(place, turns, normed, cuts, 0, buf)
    blocks = [
        (buf.at[block * length : (block + 1) * length, :], right, 0)
        for block, right in enumerate(rights)
    ]
    pair_sums(blocks, place[2], sent, kept, res)


def zone_weight(body, turns, share, length, width, args):
    return (
        functools.partial(body, turns),
        args,
        [((share, width), BF16), ((share, width), F32)],
        [((turns * length, 2 * share), BF16), ((2 * share, 256), F32)],
    )


def edge_kernel(place, d_pre, last_rows, from_next, start_row, out):
    length = d_pre.shape[0]
    quarter = length // 4
    out[...] = d_pre[...]
    row = lax.broadcasted_iota(jnp.int32, (8, 1), 0)
    one = 1.0 - start_row[:, length - 1 : length]
    two = one * (1.0 - start_row[:, length - 2 : length - 1])
    keep = jnp.where(row == 7, 1.0, jnp.where(row == 6, one, jnp.where(row == 5, two, 0.0)))
    at = pl.multiple_of((place[0] ^ 3) * quarter + quarter - 8, 8)
    out[pl.ds(at, 8), :] = (last_rows[...] + from_next[...] * keep).astype(BF16)


def stack_kernel(place, *refs):
    stack(refs[:-1], refs[-1])


def natural_kernel(row, place, own, side, other_own, other_side, out):
    quarter = out.shape[0] // 4
    for p, ref in enumerate((own, side, other_own, other_side)):
        to = pl.multiple_of((place[0] ^ p) * quarter, quarter)
        out[pl.ds(to, quarter), :] = ref[row : row + quarter, :].astype(F32)


def settle_kernel(place, kept, got, out_0, out_1, out_2):
    at = 0
    for out in (out_0, out_1, out_2):
        width = out.shape[1]
        out[...] = kept[:, at : at + width] + got[:, at : at + width].astype(F32)
        at += width


def low_kernel(place, d_low, normed, pack, first, second, outnorm, squared, out):
    out[0:RANK, :] = dot(d_low[...], normed[...])
    out[RANK:, :] = pack[...]
    out[RANK + 5 : RANK + 6, :] = first[...]
    out[RANK + 6 : RANK + 7, :] = second[...]
    out[RANK + 7 : RANK + 8, 0:DV] = outnorm[...]
    out[RANK + 7 : RANK + 8, DV : 2 * DV] = jnp.broadcast_to(squared[...], (1, DV))


def unpack_kernel(share, place, summed, query_out, key_out, value_out, up_out, bias_out, down_out):
    for row in range(TAPS):
        at = (row % 2) * (2 * DK + DV)
        line = summed[RANK + row // 2 : RANK + 1 + row // 2, :]
        query_out[row : row + 1, :] = line[:, at : at + DK]
        key_out[row : row + 1, :] = line[:, at + DK : at + 2 * DK]
        value_out[row : row + 1, :] = line[:, at + 2 * DK : at + 2 * DK + DV]
    per = D // DK
    for row in range(RANK):
        at = (row % per) * DK
        up_out[row : row + 1, :] = summed[RANK + 2 + row // per : RANK + 3 + row // per, at : at + DK]
    bias_out[...] = summed[RANK + 4 : RANK + 5, 0:DK]
    pair = 2 * share
    both = summed[0:RANK, pl.ds(pl.multiple_of(place[1] * pair, pair), pair)]
    down_out[...] = jnp.where(place[2] == 0, both[:, 0:share], both[:, share:])


COST = {
    "state_kernel": 2.3,
    "output_kernel": 2.0,
    "gate_back_kernel": 2.0,
    "mixer_back_kernel": 4.5,
    "rows_kernel": 2.8,
    "gate_kernel": 5.0,
    "gate_back_kernel_rows": 3.0,
    "far_back_kernel": 4.0,
    "far_weight_kernel": 2.5,
    "both_kernel": 3.0,
    "pre_kernel": 2.0,
    "natural_kernel": 2.0,
}


def on_device(
    block_input,
    first_gain,
    query_weight,
    key_weight,
    value_weight,
    query_conv,
    key_conv,
    value_conv,
    lowrank_down,
    lowrank_up,
    decay_bias,
    outgate_weight,
    outnorm_gain,
    output_weight,
    second_gain,
    gate_weight,
    up_weight,
    down_weight,
    starts,
    valid_mask,
    cotangent,
    teacher,
):
    length = block_input.shape[0]
    quarter, half = length // 4, length // 2
    places = lax.axis_size("seq")
    turns = places // 2
    share = D // places
    pair = 2 * share
    hidden_units = gate_weight.shape[1]
    channels = 2 * DK + DV
    seq, head = lax.axis_index("seq"), lax.axis_index("head")
    mine = (head % 2) * 2 + head // 2
    zone, side = seq // 2, seq % 2
    place = jnp.stack([mine, zone, side]).astype(jnp.int32)
    loss_weight = float(length * places * D // 8)
    row_shape = (quarter, D)
    window_shape = (DK + 16, 2 * DK)
    roomy = 6 if turns <= 4 else 20


    waiting = []

    def run(body, args, outs, scratch=(), vmem=6):
        micros = COST.get(getattr(body, "func", body).__name__, 1.0)
        gate = after(place, *waiting) if waiting else place
        made = call(body, gate, args, outs, scratch, vmem, micros)
        waiting[:] = [made[-1]]
        return made

    def hold(*xs):
        waiting.extend(xs)
        return xs[0] if len(xs) == 1 else xs

    def ready(x):
        return after(x, *waiting)

    def fold(sent, kept):
        got = flip(sent, "head", 1)
        return run(fold_kernel, [kept, got], [(row_shape, F32), (row_shape, BF16)])

    def quarters(own_rows, side_rows):
        return [own_rows, side_rows, flip(own_rows, "head", 1), flip(side_rows, "head", 1)]

    start_row = starts.astype(F32).reshape(1, length)
    input_float = block_input.astype(F32)
    normed = (input_float * root_scale(input_float) * first_gain).astype(BF16)
    pre_k = dot(normed, key_weight).astype(BF16)
    pre_v = dot(normed, value_weight).astype(BF16)
    pre_q = dot(normed, query_weight).astype(BF16)
    last_start, before_last = start_row[0, length - 1], start_row[0, length - 2]
    keep_one = 1.0 - last_start
    tail_keep = jnp.concatenate(
        [jnp.zeros((5,), F32), jnp.stack([keep_one * (1.0 - before_last), keep_one, jnp.ones((), F32)])]
    )
    tails = jnp.concatenate([pre_q[length - 8 :], pre_k[length - 8 :], pre_v[length - 8 :]], axis=1)
    edge = shift(tails * tail_keep[:, None].astype(BF16), "seq", 1)
    taps = jnp.concatenate([query_conv, key_conv, value_conv], axis=1)
    low_rank = dot(normed, lowrank_down).astype(BF16)
    u, v, x, logit, window = run(
        state_kernel,
        [pre_q, pre_k, pre_v, edge, taps, start_row, low_rank, lowrank_up, decay_bias.reshape(1, DK)],
        [
            ((length, channels), F32),
            ((length, DV), BF16),
            ((length, DK), F32),
            ((length, DK), F32),
            (window_shape, BF16),
        ],
        [((length + 8, channels), F32)],
    )

    def carry(window, sign, beside):
        found = None
        step, at = 1, 0
        while step < places:
            last = 2 * step >= places
            got = shift(window, "seq", sign * step)
            got, *_ = beside(at, step, got, window)
            args = [got] + ([] if last else [window]) + ([] if found is None else [found])
            outs = [((DK, DV), BF16)] if last else [(window_shape, BF16), (window_shape, BF16)]
            made = run(functools.partial(carry_kernel, found is None, last), args, outs)
            if not last:
                window, found = made
            step, at = 2 * step, at + 1
        return made[0]

    def finish(blocks):
        while len(blocks) < turns - 1:
            blocks.append(turn(blocks[-1], 1))
        return blocks

    valid_float = valid_mask.astype(F32)
    counts, outgates = [jnp.full((8, 128), jnp.sum(valid_float), F32)], []

    def with_forward(at, step, got, window):
        count = after(counts[-1], window)
        beside = [count + flip(count, "seq", step)]
        if at == 0:
            beside.append(dot(after(normed, window), outgate_weight))
        got, *beside = join(got, *beside)
        counts.append(beside[0])
        outgates.extend(beside[1:])
        return (got,)

    state_in = carry(window, 1, with_forward)
    outgate, valid_count = outgates[0], counts[-1]
    gain_row = outnorm_gain.reshape(1, DV)
    second_row = second_gain.reshape(1, D)
    first_row = first_gain.reshape(1, D)
    valid_row = valid_float.reshape(1, length)
    steps = [("seq", bit) for bit in (1 << p for p in range(16)) if bit < places]
    gated, mixed, scores, sent, kept = run(
        output_kernel,
        [u, v, x, start_row, state_in, outgate, gain_row, output_weight],
        [
            ((length, DV), BF16),
            ((length, DV), F32),
            ((length, length), BF16),
            ((half, D), BF16),
            ((half, D), F32),
        ],
    )

    near, far = fold(sent, kept)
    far, turned = join(far, gated)
    far, gated_1 = join(flip(far, "head", 2), turn(turned, 1))
    hidden, ffn_own = run(
        hidden_kernel, [near, far, block_input, second_row], [(row_shape, F32), (row_shape, BF16)]
    )
    ffn_side, ffn_1 = join(flip(ffn_own, "head", 2), turn(ffn_own, 1))
    ffn_in = quarters(ffn_own, ffn_side)
    activated, gate_in, up_in = run(*gate_up(ffn_in, gate_weight, up_weight))
    sent, kept = run(*rows_times([activated], [(0, 0, hidden_units, down_weight)]))
    near, far = fold(sent, kept)
    far, turned = join(far, ffn_1)
    far, ffn_2 = join(flip(far, "head", 2), turn(turned, 1))
    output_own, d_out, d_ffn_own, squared = run(
        functools.partial(loss_kernel, loss_weight),
        [near, far, hidden, teacher, cotangent, valid_row, valid_count],
        [(row_shape, BF16), (row_shape, F32), (row_shape, BF16), ((1, 1), F32)],
    )
    d_ffn_own, turned, turned_too = join(d_ffn_own, ffn_2, gated_1)
    d_ffn_side, ffn_3, gated_2 = join(
        flip(d_ffn_own, "head", 2), turn(turned, 1), turn(turned_too, 1)
    )
    d_ffn = quarters(d_ffn_own, d_ffn_side)
    d_gate, d_up = run(*gate_back_rows(d_ffn, down_weight, gate_in, up_in))
    ffn_turns = [ffn_own, *finish([ffn_1, ffn_2, ffn_3])]
    (ffn_far,) = run(stack_kernel, ffn_turns[1:], [(((turns - 1) * quarter, D), BF16)])
    sent, kept = run(
        *rows_times(
            [d_gate, d_up],
            [(0, 0, hidden_units, gate_weight), (1, 0, hidden_units, up_weight)],
        )
    )
    near, far = fold(sent, kept)
    far, turned = join(far, d_ffn_own)
    far, d_1 = join(flip(far, "head", 2), turn(turned, 1))
    d_hidden, d_branch_own, second_part, *cuts = run(
        functools.partial(hidden_back_kernel, turns),
        [near, far, hidden, d_out, second_row, normed],
        [(row_shape, F32), (row_shape, BF16), ((1, D), F32)]
        + [((quarter, 2 * pair), BF16)] * (turns - 1),
    )
    d_branch_own, turned, turned_too = join(d_branch_own, d_1, gated_2)
    d_branch_side, d_2, gated_3 = join(
        flip(d_branch_own, "head", 2), turn(turned, 1), turn(turned_too, 1)
    )
    gated_turns = finish([gated_1, gated_2, gated_3])
    d_branch = quarters(d_branch_own, d_branch_side)

    d_outgate, d_mixed, outnorm_part, direct = run(
        gate_back_kernel,
        [*d_branch, output_weight, mixed, outgate, gain_row, u, x, start_row],
        [((length, DV), BF16), ((length, DV), BF16), ((1, DV), F32), (window_shape, BF16)],
        [((length, D), BF16)],
    )
    (d_far,) = run(stack_kernel, [d_1, d_2], [((half, D), BF16)])

    d_turns, d_sides, cuts_got, outgate_turns = [d_ffn_own, d_1, d_2], [d_ffn_side], [], []
    made, grads, sums, held = [], [], {}, {}

    def weigh(name, lefts, rights):
        sums[name] = run(*far_weight(share, lefts, rights))

    def with_back(at, step, got, window):
        if at == 0:
            got, third, sides = join(
                got, turn(after(d_2, window), 1), flip(after(ffn_far, d_branch_side), "head", 2)
            )
            d_turns.append(third)
            held["ffn"] = sides
        elif at == 1:
            sides = flip(after(d_far, window), "head", 2)
            right = turn(after(d_outgate, window), 1)
            made.append(
                run(
                    *far_gate_up(ffn_turns, [ffn_side, held["ffn"]], gate_weight, up_weight, pair),
                    vmem=roomy,
                )
            )
            got, sides, right = join(got, sides, right)
            d_sides.append(sides)
            outgate_turns.append(right)
        elif at == 2:
            side = flip(after(d_turns[3], window), "head", 2)
            other = flip(after(made[0][4], window), "head", 1)
            made.append(run(*gate_up([other], gate_weight, up_weight, pair), vmem=roomy))
            right = turn(after(outgate_turns[-1], made[1][3]), 1)
            got, side, right = join(got, side, right)
            d_sides.append(side)
            outgate_turns.append(right)
            for extra in range(4, turns):
                d_turns.append(turn(d_turns[-1], 1))
                d_sides.append(flip(d_turns[-1], "head", 2))
        return (got,)

    later = carry(direct, -1, with_back)
    d_pre, last_rows, pack, d_low, back_rows = run(
        mixer_back_kernel,
        [
            d_mixed, state_in, later, u, v, x, scores, pre_q, pre_k, pre_v, edge, taps,
            logit, start_row, low_rank, lowrank_up,
        ],
        [
            ((length, channels), BF16),
            ((8, channels), F32),
            ((8, D), F32),
            ((RANK, length), F32),
            ((8, channels), F32),
        ],
        [
            ((length + 8, channels), F32),
            ((length + 8, channels), F32),
            ((16, DK), F32),
            ((length, DK), F32),
        ],
        vmem=7,
    )

    grads.append(
        run(
            *far_back_rows(d_turns, d_sides, down_weight, made[0][1], made[0][2], pair), vmem=roomy
        )
    )
    from_next, d_low_got, right, rows_other = join(
        shift(back_rows, "seq", -1),
        flip(d_low, "head", 1),
        turn(after(outgate_turns[-1], back_rows), 1),
        flip(grads[0][3], "head", 1),
    )
    outgate_turns = finish([*outgate_turns, right])
    hold(from_next)
    (d_pre,) = run(
        edge_kernel, [d_pre, last_rows, from_next, start_row], [((length, channels), BF16)]
    )

    pre_1 = turn(d_pre, 1)
    d_low = d_low + d_low_got
    grads.append(
        run(*gate_back_rows([rows_other], down_weight, made[1][1], made[1][2], pair), vmem=roomy)
    )
    cuts_in = [part[3] for part in made]
    weigh("gate", cuts_in, [grad[0] for grad in grads])
    pre_1, gate_sent, d_low_got = join(pre_1, sums["gate"][0], flip(d_low, "head", 2))

    pre_2 = turn(pre_1, 1)
    gate_got = flip(gate_sent, "seq", 1)
    cuts_got = [turn(after(cuts[by - 1], pre_1), by) for by in range(1, turns)]
    hold(pre_1)
    sent, kept = run(
        *rows_times(
            [d_outgate, d_pre],
            [
                (0, 0, DV, outgate_weight),
                (1, 0, DK, query_weight),
                (1, DK, DK, key_weight),
                (1, 2 * DK, DV, value_weight),
            ],
        )
    )
    near, far = fold(sent, kept)
    far = flip(far, "head", 2)
    weigh("up", cuts_in, [grad[1] for grad in grads])
    weigh("down", [grad[2] for grad in grads], [part[0] for part in made])
    grad_own, first_part, d_lowrank = run(
        input_back_kernel,
        [near, far, block_input, d_hidden, first_row, d_low, d_low_got, lowrank_down.T],
        [(row_shape, BF16), ((1, D), F32), ((RANK, length), BF16)],
    )
    (small,) = run(
        low_kernel,
        [d_lowrank, normed, pack, first_part, second_part, outnorm_part, squared],
        [((RANK + 8, D), F32)],
    )
    (rows_both,) = run(stack_kernel, [grad_own, output_own], [((half, D), BF16)])
    pre_2, gate_got, small, rows_both, up_sent, down_sent, *cuts_got = join(
        pre_2, gate_got, small, rows_both, sums["up"][0], sums["down"][0], *cuts_got
    )
    (cuts_near,) = run(stack_kernel, cuts_got, [(((turns - 1) * quarter, 2 * pair), BF16)])

    pre_3 = turn(pre_2, 1)
    cuts_side = flip(cuts_near, "head", 2)
    cuts_far = quarters(cuts_near, cuts_side)
    up_got = flip(up_sent, "seq", 1)
    rows_side = flip(rows_both, "head", 2)
    pre_3, up_got, down_sent, *cuts_far = join(pre_3, up_got, down_sent, *cuts_far)
    small = total(after(small, pre_3), steps[:1])
    down_got = flip(down_sent, "seq", 1)
    sum_pre = run(
        *zone_weight(
            pre_kernel, turns, share, length, channels,
            [normed, *cuts_far, d_pre, *finish([pre_1, pre_2, pre_3])],
        )
    )
    pre_got = flip(sum_pre[0], "seq", 1)
    sum_both = run(
        *zone_weight(
            both_kernel, turns, share, length, 2 * DV,
            [*d_branch, normed, *cuts_far, d_outgate, gated, *outgate_turns, *gated_turns],
        )
    )
    both_got = flip(sum_both[0], "seq", 1)
    small = total(after(small, sum_pre[0]), steps[1:])
    shared = total(small[RANK + 5 :], [("head", 1), ("head", 2)])
    grad_query, grad_key, grad_value = run(
        settle_kernel, [sum_pre[1], pre_got],
        [((share, DK), F32), ((share, DK), F32), ((share, DV), F32)],
    )
    both_other, side_other = flip(rows_both, "head", 1), flip(rows_side, "head", 1)
    (grad_input,) = run(
        functools.partial(natural_kernel, 0),
        [rows_both, rows_side, both_other, side_other],
        [((length, D), F32)],
    )
    (block_output,) = run(
        functools.partial(natural_kernel, quarter),
        [rows_both, rows_side, both_other, side_other],
        [((length, D), F32)],
    )
    grad_gate, grad_up, grad_down, grad_both = (
        after(kept, sum_pre[0]) + got.astype(F32)
        for got, kept in (
            (gate_got, sums["gate"][1]),
            (up_got, sums["up"][1]),
            (down_got, sums["down"][1]),
            (both_got, sum_both[1]),
        )
    )
    grad_output, grad_outgate = grad_both[:, :DV], grad_both[:, DV:]
    apart = small
    taps_query, taps_key, taps_value, grad_lowrank_up, bias_row, down_row = run(
        functools.partial(unpack_kernel, share),
        [apart],
        [
            ((TAPS, DK), F32),
            ((TAPS, DK), F32),
            ((TAPS, DV), F32),
            ((RANK, DK), F32),
            ((1, DK), F32),
            ((RANK, share), F32),
        ],
    )
    distill = shared[2, DV] / (valid_count[0, 0] * D)
    return (
        block_output,
        distill,
        grad_input,
        shared[0],
        grad_query,
        grad_key,
        grad_value,
        taps_query,
        taps_key,
        taps_value,
        down_row.T,
        grad_lowrank_up,
        bias_row.reshape(DK),
        grad_outgate,
        shared[2, :DV],
        grad_output,
        shared[1],
        grad_gate,
        grad_up,
        grad_down,
    )


def solution(mesh):
    rows, cols, whole = P("seq", None), P(None, "head"), P()
    in_specs = (
        rows, whole, cols, cols, cols, cols, cols, cols, whole, cols, P("head"), cols, whole, cols,
        whole, cols, cols, cols, P("seq"), P("seq"), rows, rows,
    )
    tiles = P("seq", "head")
    out_specs = (
        rows, whole, rows, whole, tiles, tiles, tiles, cols, cols, cols, rows, cols, P("head"), tiles,
        whole, tiles, whole, tiles, tiles, tiles,
    )
    return jax.shard_map(
        on_device, mesh=mesh, in_specs=in_specs, out_specs=out_specs, check_vma=False
    )
```
